256 devices in a mesh: grp: 8 (over z_hi, y), sp: 32 (over z_lo, x, core).
Axes of the slice: x: 4, y: 4, z: 8 (z_hi: 2, z_lo: 4; z = z_hi * 4 + z_lo), core: 2. Of those that a mesh axis runs over, the one named last changes fastest.
Arguments:
- alpha: float32 [80, 32, 4096], P('grp', None, 'sp'), may hold values from -6 to 6
- ensemble: bfloat16 [80, 3, 32, 4096], P('grp', None, None, 'sp'), may hold values from -6 to 6
- static_std: float32 [3, 32, 4096], P(None, 'grp', 'sp'), may hold values from 0.2 to 1
- control: float32 [3, 32, 4096], P(None, 'grp', 'sp'), may hold values from -6 to 6
- loc_spectrum: float32 [1024], replicated, may hold values from 0.00024414062 to 0.001953125
- obs_cell: int32 [262144], P(('grp', 'sp')), may hold values from 0 to 131071, as said below
- obs_step: int32 [262144], P(('grp', 'sp')), may hold values from 0 to 2
- innovation: float32 [262144], P(('grp', 'sp')), may hold values from -6 to 6
- obs_weight: float32 [262144], P(('grp', 'sp')), may hold values from 0.5 to 4
Outputs:
- grad_alpha: float32 [80, 32, 4096], P('grp', None, 'sp')
- grad_control: float32 [3, 32, 4096], P(None, 'grp', 'sp')
The draws below stay inside these ranges and needn't reach their ends.
Inputs may be any that keep to these rules, and one draw needn't show every extreme that they name: `obs_cell`: an entry is row * 4096 + column. Entries 1024 * b to 1024 * (b + 1) - 1 lie in the tile of 4 rows from row 4 * (b // 32) and 128 columns from column 128 * (b % 32).
All inputs are finite; a program needn't handle non-finite values.
Results may differ from the reference program's by a relative error of at most 0.0075.
Values may be sent and summed in bfloat16 or wider, within the bound.
No kernel may reach another device: no remote copies, remote signals or barrier semaphores. Data moves between devices by JAX's collectives and lax.ppermute only.
A program may use at most 128 MiB of HBM per device.

```python
import math
import jax
import jax.numpy as jnp
from jax import lax

NX = 4096
KEEP = 1024
STEPS = 2
OBS_DEV = 1024
MEMBERS = 80
NY = 32
TILE_ROWS = 4
TILE_COLS = 128
OBS = 262144


def draw_obs_cell(key, part):
    base = jax.random.fold_in(key, 11)
    row_key, col_key = jax.random.split(base)
    blocks = jnp.arange(OBS, dtype=jnp.int32) // OBS_DEV
    col_blocks = NX // TILE_COLS
    block_row = blocks // col_blocks
    block_col = blocks % col_blocks
    local_row = jax.random.randint(row_key, (OBS,), 0, TILE_ROWS, dtype=jnp.int32)
    local_col = jax.random.randint(col_key, (OBS,), 0, TILE_COLS, dtype=jnp.int32)
    return ((block_row * TILE_ROWS + local_row) * NX + block_col * TILE_COLS + local_col).astype(jnp.int32)


def plant(result, key, low, high):
    spot = [jax.random.randint(jax.random.fold_in(key, axis), (), 0, length) for axis, length in enumerate(result.shape)]
    main_axis = result.shape.index(max(result.shape))
    beside = spot[:main_axis] + [(spot[main_axis] + 1) % result.shape[main_axis]] + spot[main_axis + 1:]
    return result.at[tuple(spot)].set(low).at[tuple(beside)].set(high)


def strengthened(array, rng, source, target, parts, factor):
    def block_of(dim):
        return (jnp.arange(array.shape[dim]) // (array.shape[dim] // parts)).reshape((-1,) + (1,) * (array.ndim - 1 - dim))

    one_side = jax.random.permutation(rng, parts)[block_of(target)]
    other_side = (block_of(target) + parts // 2) % parts
    return jnp.where((block_of(source) == one_side) | (block_of(source) == other_side), factor * array, array)


def block_scale(key, extent, shards, low, high):
    def one(axis_at, blocks):
        draws = jax.random.uniform(jax.random.fold_in(jax.random.fold_in(key, 6), axis_at), (blocks,), jnp.float32, low / len(shards), high / len(shards))
        return jnp.repeat(jnp.exp(draws), extent[axis_at] // blocks).reshape((-1,) + (1,) * (len(extent) - axis_at - 1))

    level = one(*shards[0])
    for cut in shards[1:]:
        level = level * one(*cut)
    return level


def centred(stream_key, shape, scale, limit, pieces=(), kind=jnp.bfloat16):
    drawn = jax.random.normal(stream_key, shape, jnp.float32) * scale
    if len(pieces) > 0:
        drawn = block_scale(stream_key, shape, pieces, -0.22, 0.18) * drawn
    return jnp.clip(drawn, min=-limit, max=limit).astype(kind)


def noise_with(key, dims, scale, limit, pieces, heavy, held_as=jnp.bfloat16):
    array = scale * jax.random.normal(key, dims, jnp.float32)
    if pieces:
        array = array * block_scale(key, dims, pieces, -0.22, 0.18)
    return jnp.clip(strengthened(array, jax.random.fold_in(key, 3), *heavy), -limit, limit).astype(held_as)


def setup_inputs(seed: int = 0) -> dict:
    key_of = jax.random.split(jax.random.key(seed), 10)
    alpha = centred(key_of[0], (MEMBERS, NY, NX), 1.0, 6.0, ((0, 8), (2, 32)), jnp.float32)
    ensemble = noise_with(key_of[1], (MEMBERS, 3, NY, NX), 1.0, 6.0, ((0, 8), (3, 32)), (0, 2, 8, 2.0))
    static_std = jnp.clip(jnp.exp(math.log(1.0) - 1.609438 * jax.random.uniform(key_of[2], (3, NY, NX), jnp.float32) ** block_scale(key_of[2], (3, NY, NX), ((1, 8), (2, 32)), -0.2, 0.2)), 0.2, 1.0)
    control = centred(key_of[3], (3, NY, NX), 1.0, 6.0, ((1, 8), (2, 32)), jnp.float32)
    loc_spectrum = jnp.clip(jnp.exp(jax.random.uniform(key_of[4], (KEEP,), jnp.float32, math.log(0.00024414062), math.log(0.001953125))), 0.00024414062, 0.001953125)
    obs_cell = draw_obs_cell(jax.random.fold_in(key_of[9], 71), 0)
    obs_step = plant(jax.random.randint(key_of[6], (OBS,), 0, STEPS + 1), jax.random.fold_in(key_of[6], 1), 0, STEPS).astype(jnp.int32)
    innovation = centred(key_of[7], (OBS,), 1.0, 6.0, ((0, 256),), jnp.float32)
    obs_weight = jnp.clip(jnp.exp(math.log(4.0) - 2.0794415 * jax.random.uniform(key_of[8], (OBS,), jnp.float32) ** block_scale(key_of[8], (OBS,), ((0, 256),), -0.2, 0.2)), 0.5, 4.0)
    return {"alpha": alpha, "ensemble": ensemble, "static_std": static_std, "control": control, "loc_spectrum": loc_spectrum, "obs_cell": obs_cell, "obs_step": obs_step, "innovation": innovation, "obs_weight": obs_weight}


courant = 0.4

def spectral_filter(rows_data, loc_spectrum):
    length_x = rows_data.shape[1]
    kept_waves = loc_spectrum.shape[0]
    freq_block = math.gcd(kept_waves, 256)
    positions = jnp.arange(length_x, dtype=jnp.int32)
    filtered = jnp.zeros(rows_data.shape, jnp.float32)
    for start_wave in range(0, kept_waves, freq_block):
        waves = start_wave + jnp.arange(freq_block, dtype=jnp.int32)
        phases = positions[:, None] * waves[None, :] % length_x
        radians = 2.0 * math.pi / length_x * phases.astype(jnp.float32)
        fourier_basis = jnp.concatenate([jnp.cos(radians), jnp.sin(radians)], axis=1)
        weights = loc_spectrum[start_wave:start_wave + freq_block]
        weights = jnp.concatenate([weights, weights])
        coeffs = jnp.dot(rows_data, fourier_basis, precision=lax.Precision.HIGHEST, preferred_element_type=jnp.float32)
        filtered = filtered + jnp.dot(coeffs * weights[None, :], fourier_basis.T, precision=lax.Precision.HIGHEST, preferred_element_type=jnp.float32)
    return filtered

def diff_x(field):
    return 0.5 * (jnp.roll(field, -1, axis=-1) - jnp.roll(field, 1, axis=-1))

def diff_y(field):
    padded = jnp.pad(field, ((1, 1), (0, 0)))
    return 0.5 * (padded[2:] - padded[:-2])

def coriolis():
    rows_index = jnp.arange(NY, dtype=jnp.int32).astype(jnp.float32)
    return (0.1 + 0.2 * (rows_index + 0.5) / NY)[:, None]

def model_step(state, rotation):
    height, eastward, northward = (state[0], state[1], state[2])
    new_height = height - courant * (diff_x(eastward) + diff_y(northward))
    new_east = eastward - courant * diff_x(new_height) + rotation * northward
    new_north = northward - courant * diff_y(new_height) - rotation * eastward
    return jnp.stack([new_height, new_east, new_north])

def adjoint_step(state, rotation):
    back_h, back_u, back_w = (state[0], state[1], state[2])
    adj_height = back_h + courant * (diff_x(back_u) + diff_y(back_w))
    adj_east = back_u - rotation * back_w + courant * diff_x(adj_height)
    adj_north = back_w + rotation * back_u + courant * diff_y(adj_height)
    return jnp.stack([adj_height, adj_east, adj_north])

def reference(alpha, ensemble, static_std, control, loc_spectrum, obs_cell, obs_step, innovation, obs_weight):
    spread = 1.0 / math.sqrt(MEMBERS - 1)
    rotation = coriolis()
    localized = spectral_filter(alpha.reshape(MEMBERS * NY, NX), loc_spectrum).reshape(alpha.shape).astype(jnp.bfloat16)
    partial_value = jnp.einsum('mvyx,myx->vyx', ensemble.astype(jnp.float32), localized.astype(jnp.float32), precision=lax.Precision.HIGHEST)
    increment = static_std * control + spread * partial_value
    first_state = model_step(increment, rotation)
    second_state = model_step(first_state, rotation)
    states = (increment, first_state, second_state)
    observed = jnp.zeros(innovation.shape, jnp.float32)
    for moment in range(3):
        values = states[moment][0].reshape(-1)[obs_cell]
        observed = jnp.where(obs_step == moment, values, observed)
    misfit = obs_weight * (observed - innovation)
    zero_field = jnp.zeros((NY, NX), jnp.float32)
    forcings = []
    for moment in range(3):
        spread_obs = jnp.where(obs_step == moment, misfit, jnp.zeros_like(misfit))
        height_force = jnp.zeros((NY * NX,), jnp.float32).at[obs_cell].add(spread_obs).reshape(NY, NX)
        forcings.append(jnp.stack([height_force, zero_field, zero_field]))
    adjoint = adjoint_step(forcings[2], rotation) + forcings[1]
    adjoint = adjoint_step(adjoint, rotation) + forcings[0]
    grad_control = control + static_std * adjoint
    half = adjoint.astype(jnp.bfloat16)
    weighted = jnp.einsum('mvyx,vyx->myx', ensemble.astype(jnp.float32), half.astype(jnp.float32), precision=lax.Precision.HIGHEST)
    grad_alpha = alpha + spread * spectral_filter(weighted.reshape(MEMBERS * NY, NX), loc_spectrum).reshape(alpha.shape)
    return (grad_alpha, grad_control)
```

```python
import math

import jax
import jax.numpy as jnp
import numpy as np
from jax import lax
from jax.experimental import pallas as pl
from jax.experimental.pallas import tpu as pltpu
from jax.sharding import Mesh
from jax.sharding import PartitionSpec as P

GRP_SP = ("grp", "sp_0", "sp_1", "sp_2")
SP = ("sp_0", "sp_1", "sp_2")

MEM = 10
SLOTS = 16
ROWS = 32
COLS = 128
BLOCKS = 32
GROUPS = 8
TILE_ROWS = 4
NX = BLOCKS * COLS
KEEP = 1024
ALPHAS = 2 * KEEP // BLOCKS
FIELDS = 9
COURANT = 0.4

F32 = jnp.float32
BF16 = jnp.bfloat16
VMEM = pltpu.VMEM


def call(body, out_shape, scratch=(), n_in=1):
    single = not isinstance(out_shape, (list, tuple))
    spec = pl.BlockSpec(memory_space=VMEM)
    return pl.pallas_call(
        body,
        out_shape=out_shape,
        in_specs=[spec] * n_in,
        out_specs=spec if single else [spec] * len(out_shape),
        scratch_shapes=list(scratch),
        compiler_params=pltpu.CompilerParams(vmem_limit_bytes=32 << 20),
    )


def split(table):
    high = table.astype(jnp.bfloat16)
    low = (table - np.asarray(high).astype(np.float64)).astype(jnp.bfloat16)
    return np.asarray(high), np.asarray(low)


def tables():
    j = np.arange(COLS)
    wave = np.concatenate([np.arange(ALPHAS // 2), -1 - np.arange(ALPHAS // 2)])
    angle = 2.0 * np.pi * ((j[:, None] * wave[None, :]) % COLS) / COLS
    c, s = np.cos(angle), np.sin(angle)
    basis = np.concatenate(
        [np.concatenate([c, -s], axis=1), np.concatenate([s, c], axis=1)], axis=0
    )
    turn = 2.0 * np.pi * np.arange(BLOCKS)[:, None] * j[None, :] / NX
    twiddle = np.stack([np.cos(turn), np.sin(turn)]).astype(np.float32)
    high, low = split(basis)
    return high, low, np.ascontiguousarray(high.T), np.ascontiguousarray(low.T), twiddle


def fft(load, start, step, n, sign):
    if n == 1:
        return [load(start)]
    even = fft(load, start, 2 * step, n // 2, sign)
    odd = fft(load, start + step, 2 * step, n // 2, sign)
    low, high = [], []
    for k in range(n // 2):
        er, ei = even[k]
        xr, xi = odd[k]
        if k == 0:
            tr, ti = xr, xi
        elif 4 * k == n:
            tr, ti = (-xi, xr) if sign > 0 else (xi, -xr)
        elif 8 * k == n:
            r = math.sqrt(0.5)
            tr, ti = ((xr - xi) * r, (xr + xi) * r) if sign > 0 else ((xr + xi) * r, (xi - xr) * r)
        elif 8 * k == 3 * n:
            r = math.sqrt(0.5)
            tr, ti = (-(xr + xi) * r, (xr - xi) * r) if sign > 0 else ((xi - xr) * r, -(xr + xi) * r)
        else:
            c = math.cos(2.0 * math.pi * k / n)
            s = sign * math.sin(2.0 * math.pi * k / n)
            tr, ti = xr * c - xi * s, xr * s + xi * c
        low.append((er + tr, ei + ti))
        high.append((er - tr, ei - ti))
    return low + high


def product(x, high, low):
    xh = x.astype(BF16)
    xl = (x - xh.astype(F32)).astype(BF16)
    h = high[...]
    total = jnp.dot(xl, h, preferred_element_type=F32)
    total = total + jnp.dot(xh, low[...], preferred_element_type=F32)
    return total + jnp.dot(xh, h, preferred_element_type=F32)


def filter_rows(rows, high, low, high_t, low_t, twiddle, weights, out, wide, spec):
    def load(p):
        x = rows[p].astype(F32)
        return x[:8], x[8:]

    for b, (ur, ui) in enumerate(fft(load, 0, 1, BLOCKS, -1)):
        c, s = twiddle[0, b : b + 1, :], twiddle[1, b : b + 1, :]
        wide[8 * b : 8 * b + 8, :COLS] = ur * c + ui * s
        wide[8 * b : 8 * b + 8, COLS:] = ui * c - ur * s
    spec[...] = product(wide[...], high, low)
    for b in range(BLOCKS):
        spec[8 * b : 8 * b + 8, :] = spec[8 * b : 8 * b + 8, :] * weights[b : b + 1, :]
    wide[...] = product(spec[...], high_t, low_t)

    def load_back(b):
        c, s = twiddle[0, b : b + 1, :], twiddle[1, b : b + 1, :]
        yr, yi = wide[8 * b : 8 * b + 8, :COLS], wide[8 * b : 8 * b + 8, COLS:]
        return yr * c - yi * s, yr * s + yi * c

    for p, (yr, yi) in enumerate(fft(load_back, 0, 1, BLOCKS, 1)):
        out[p] = jnp.concatenate([yr, yi], axis=0).astype(BF16)


def localize(rows, weights):
    return call(
        filter_rows,
        jax.ShapeDtypeStruct((BLOCKS, SLOTS, COLS), BF16),
        [VMEM((8 * BLOCKS, 2 * COLS), F32), VMEM((8 * BLOCKS, COLS), F32)],
        7,
    )(rows, *tables(), weights)


def by_row(flat, out):
    for y in range(ROWS):
        x = flat[pl.ds(y, MEM, stride=ROWS), :]
        x = jnp.concatenate([x, jnp.zeros((SLOTS - MEM, COLS), F32)], axis=0)
        out[y] = x.astype(BF16)


def to_send(alpha):
    return call(by_row, jax.ShapeDtypeStruct((ROWS, SLOTS, COLS), BF16))(
        alpha.reshape(MEM * ROWS, COLS)
    )


def contract(ensemble, arrived, out, flat):
    flat[...] = arrived[...].astype(F32).reshape(ROWS * SLOTS, COLS)
    totals = [jnp.zeros((ROWS, COLS), F32)] * 3
    for m in range(MEM):
        field = flat[pl.ds(m, ROWS, stride=SLOTS), :]
        for v in range(3):
            totals[v] = totals[v] + ensemble[m, v].astype(F32) * field
    for v in range(3):
        part = totals[v].astype(BF16)
        for g in range(GROUPS):
            out[g, ROWS * v : ROWS * v + ROWS, :] = part


def partial_sums(ensemble, arrived):
    return call(
        contract,
        jax.ShapeDtypeStruct((GROUPS, 3 * ROWS, COLS), BF16),
        [VMEM((ROWS * SLOTS, COLS), F32)],
        2,
    )(ensemble, arrived)


def observe(cell, step, innovation, weight, std, control, out):
    where_row = jnp.right_shift(cell[...], 12) & (TILE_ROWS - 1)
    key = step[...] * TILE_ROWS + where_row
    column = cell[...] & (COLS - 1)
    w = weight[...]
    wd = w * innovation[...]
    n = 3 * TILE_ROWS
    count = w.shape[1]
    mine = lax.broadcasted_iota(jnp.int32, (n, count), 0) == key
    values = jnp.concatenate([jnp.where(mine, w, 0.0), jnp.where(mine, wd, 0.0)], axis=0)
    high = values.astype(BF16)
    rest = values - high.astype(F32)
    mid = rest.astype(BF16)
    low = (rest - mid.astype(F32)).astype(BF16)
    hot = (lax.broadcasted_iota(jnp.int32, (COLS, count), 0) == column).astype(F32).astype(BF16)
    total = jnp.zeros((2 * n, COLS), F32)
    for piece in (low, mid, high):
        total = total + lax.dot_general(
            piece, hot, (((1,), (1,)), ((), ())), preferred_element_type=F32
        )
    for g in range(GROUPS):
        out[g, : 2 * n, :] = total
        for v in range(3):
            out[g, 2 * n + 4 * v : 2 * n + 4 * v + 4, :] = std[v] * control[v]
        out[g, 36:40, :] = jnp.zeros((4, COLS), F32)


def tile_fields(cell, step, innovation, weight, std, control):
    flat = [a.reshape(1, -1) for a in (cell, step, innovation, weight)]
    return call(observe, jax.ShapeDtypeStruct((GROUPS, 40, COLS), F32), (), 6)(
        *flat, std, control
    )


def stack_rows(arrived, out):
    for f in range(FIELDS):
        for g in range(GROUPS):
            out[f, TILE_ROWS * g : TILE_ROWS * g + TILE_ROWS, :] = arrived[
                g, TILE_ROWS * f : TILE_ROWS * f + TILE_ROWS, :
            ]


def all_rows(arrived):
    return call(stack_rows, jax.ShapeDtypeStruct((FIELDS, ROWS, COLS), F32))(arrived)


def add_groups(arrived, fields, out):
    spread = 1.0 / math.sqrt(MEM * GROUPS - 1)
    for v in range(3):
        total = arrived[0, ROWS * v : ROWS * v + ROWS, :].astype(F32)
        for g in range(1, GROUPS):
            total = total + arrived[g, ROWS * v : ROWS * v + ROWS, :].astype(F32)
        out[v] = spread * total + fields[6 + v]


def increments(arrived, fields):
    return call(add_groups, jax.ShapeDtypeStruct((3, ROWS, COLS), F32), (), 2)(arrived, fields)


def window(inc, inc_low, inc_high, fields, f_low, f_high, ensemble, sent, adj, flat):
    lane = lax.broadcasted_iota(jnp.int32, (ROWS, COLS), 1)

    def wide(main, low, high):
        rim = jnp.where(lane < 8, high, jnp.where(lane >= COLS - 8, low, 0.0))
        return jnp.concatenate([main, rim], axis=1)

    row = lax.broadcasted_iota(jnp.int32, (ROWS, 2 * COLS), 0)
    rotation = 0.1 + 0.2 * (row.astype(F32) + 0.5) / ROWS
    down = row < ROWS - 1
    up = row > 0
    half_c = 0.5 * COURANT

    def dx(q):
        return half_c * (pltpu.roll(q, 2 * COLS - 1, 1) - pltpu.roll(q, 1, 1))

    def dy(q):
        below = jnp.where(down, pltpu.roll(q, ROWS - 1, 0), 0.0)
        above = jnp.where(up, pltpu.roll(q, 1, 0), 0.0)
        return half_c * (below - above)

    def forward(h, u, w):
        h1 = h - (dx(u) + dy(w))
        return h1, u - dx(h1) + rotation * w, w - dy(h1) - rotation * u

    def backward(bh, bu, bw):
        a = bh + (dx(bu) + dy(bw))
        return a, bu - rotation * bw + dx(a), bw + rotation * bu + dy(a)

    state = tuple(wide(inc[v], inc_low[v], inc_high[v]) for v in range(3))
    forcing = []
    for t in range(3):
        w_t = wide(fields[t], f_low[t], f_high[t])
        v_t = wide(fields[3 + t], f_low[3 + t], f_high[3 + t])
        forcing.append(w_t * state[0] - v_t)
        if t < 2:
            state = forward(*state)
    zero = jnp.zeros((ROWS, 2 * COLS), F32)
    bh, bu, bw = backward(forcing[2], zero, zero)
    bh, bu, bw = backward(bh + forcing[1], bu, bw)
    bh = bh + forcing[0]
    fin = [x[:, :COLS] for x in (bh, bu, bw)]
    for v in range(3):
        adj[v] = fin[v]
    for m in range(MEM):
        total = ensemble[m, 0].astype(F32) * fin[0]
        for v in range(1, 3):
            total = total + ensemble[m, v].astype(F32) * fin[v]
        flat[ROWS * m : ROWS * m + ROWS, :] = total
    by_row(flat, sent)


def assimilate(inc, inc_low, inc_high, fields, f_low, f_high, ensemble):
    return call(
        window,
        [
            jax.ShapeDtypeStruct((ROWS, SLOTS, COLS), BF16),
            jax.ShapeDtypeStruct((3, ROWS, COLS), F32),
        ],
        [VMEM((MEM * ROWS, COLS), F32)],
        7,
    )(inc, inc_low, inc_high, fields, f_low, f_high, ensemble)


def add_alpha(alpha, arrived, out, flat):
    spread = 1.0 / math.sqrt(MEM * GROUPS - 1)
    flat[...] = arrived[...].astype(F32).reshape(ROWS * SLOTS, COLS)
    for m in range(MEM):
        out[m] = alpha[m] + spread * flat[pl.ds(m, ROWS, stride=SLOTS), :]


def finish(alpha, arrived):
    return call(
        add_alpha,
        jax.ShapeDtypeStruct((MEM, ROWS, COLS), F32),
        [VMEM((ROWS * SLOTS, COLS), F32)],
        2,
    )(alpha, arrived)


def wave_weights(loc_spectrum):
    side = KEEP // BLOCKS
    first = jnp.arange(KEEP) == 0
    up = jnp.where(first, loc_spectrum, 0.5 * loc_spectrum).reshape(side, BLOCKS)
    after = jnp.concatenate([0.5 * loc_spectrum[1:], jnp.zeros((1,), F32)])
    down = after.reshape(side, BLOCKS)[:, ::-1]
    both = jnp.concatenate([up, down], axis=0).T
    return jnp.concatenate([both, both], axis=1)


def swap(x, axis):
    return lax.all_to_all(x, axis, split_axis=0, concat_axis=0, tiled=True)


def neighbours(x):
    ahead = [(i, (i + 1) % BLOCKS) for i in range(BLOCKS)]
    back = [(t, s) for s, t in ahead]
    return lax.ppermute(x, SP, ahead), lax.ppermute(x, SP, back)


def per_device(
    alpha, ensemble, static_std, control, loc_spectrum, obs_cell, obs_step, innovation, obs_weight
):
    first_row = lax.axis_index("grp") * TILE_ROWS
    rows = swap(to_send(alpha), SP)
    tiles = tile_fields(obs_cell, obs_step, innovation, obs_weight, static_std, control)
    weights = wave_weights(loc_spectrum)
    localized = swap(localize(rows, weights), SP)
    fields = all_rows(swap(tiles, "grp"))
    f_low, f_high = neighbours(fields[:6])
    summed = swap(partial_sums(ensemble, localized), "grp")
    inc = increments(summed, fields)
    inc_low, inc_high = neighbours(inc)
    sent, adjoint = assimilate(inc, inc_low, inc_high, fields, f_low, f_high, ensemble)
    weighted = swap(sent, SP)
    mine = lax.dynamic_slice_in_dim(adjoint, first_row, TILE_ROWS, axis=1)
    grad_control = control + static_std * mine
    filtered = swap(localize(weighted, weights), SP)
    return finish(alpha, filtered), grad_control


def solution(mesh):
    torus = Mesh(mesh.devices.reshape(mesh.shape["grp"], 4, 4, 2), GRP_SP)
    placed = (
        P("grp", None, SP),
        P("grp", None, None, SP),
        P(None, "grp", SP),
        P(None, "grp", SP),
        P(),
        P(GRP_SP),
        P(GRP_SP),
        P(GRP_SP),
        P(GRP_SP),
    )
    return jax.shard_map(
        per_device,
        mesh=torus,
        in_specs=placed,
        out_specs=(P("grp", None, SP), P(None, "grp", SP)),
        check_vma=False,
    )
```

```python
import functools
import math

import jax
import jax.numpy as jnp
import numpy as np
from jax import lax
from jax.experimental import pallas as pl
from jax.experimental.pallas import tpu as pltpu
from jax.sharding import Mesh
from jax.sharding import PartitionSpec as P

GRP_SP = ("grp", "sp_0", "sp_1", "sp_2")
SP = ("sp_0", "sp_1", "sp_2")

MEM = 10
SLOTS = 16
ROWS = 32
COLS = 128
BLOCKS = 32
GROUPS = 8
TILE_ROWS = 4
NX = BLOCKS * COLS
KEEP = 1024
ALPHAS = 2 * KEEP // BLOCKS
RIM = 8
SLOT_COUNT = COLS // 16
EXTRA = MEM - SLOT_COUNT
COURANT = 0.4

F32 = jnp.float32
BF16 = jnp.bfloat16
VMEM = pltpu.VMEM


def call(body, out_shape, scratch=(), n_in=1):
    single = not isinstance(out_shape, (list, tuple))
    spec = pl.BlockSpec(memory_space=VMEM)
    return pl.pallas_call(
        body,
        out_shape=out_shape,
        in_specs=[spec] * n_in,
        out_specs=spec if single else [spec] * len(out_shape),
        scratch_shapes=list(scratch),
        compiler_params=pltpu.CompilerParams(vmem_limit_bytes=32 << 20),
    )


def split(table):
    high = table.astype(jnp.bfloat16)
    low = (table - np.asarray(high).astype(np.float64)).astype(jnp.bfloat16)
    return np.asarray(high), np.asarray(low)


def tables():
    j = np.arange(COLS)
    wave = np.concatenate([np.arange(ALPHAS // 2), -1 - np.arange(ALPHAS // 2)])
    angle = 2.0 * np.pi * ((j[:, None] * wave[None, :]) % COLS) / COLS
    c, s = np.cos(angle), np.sin(angle)
    basis = np.concatenate(
        [np.concatenate([c, -s], axis=1), np.concatenate([s, c], axis=1)], axis=0
    )
    turn = 2.0 * np.pi * np.arange(BLOCKS)[:, None] * j[None, :] / NX
    twiddle = np.stack([np.cos(turn), np.sin(turn)]).astype(np.float32)
    high, low = split(basis)
    return high, low, np.ascontiguousarray(high.T), np.ascontiguousarray(low.T), twiddle


def fft(load, start, step, n, sign):
    if n == 1:
        return [load(start)]
    even = fft(load, start, 2 * step, n // 2, sign)
    odd = fft(load, start + step, 2 * step, n // 2, sign)
    low, high = [], []
    for k in range(n // 2):
        er, ei = even[k]
        xr, xi = odd[k]
        if k == 0:
            tr, ti = xr, xi
        elif 4 * k == n:
            tr, ti = (-xi, xr) if sign > 0 else (xi, -xr)
        elif 8 * k == n:
            r = math.sqrt(0.5)
            tr, ti = ((xr - xi) * r, (xr + xi) * r) if sign > 0 else ((xr + xi) * r, (xi - xr) * r)
        elif 8 * k == 3 * n:
            r = math.sqrt(0.5)
            tr, ti = (-(xr + xi) * r, (xr - xi) * r) if sign > 0 else ((xi - xr) * r, -(xr + xi) * r)
        else:
            c = math.cos(2.0 * math.pi * k / n)
            s = sign * math.sin(2.0 * math.pi * k / n)
            tr, ti = xr * c - xi * s, xr * s + xi * c
        low.append((er + tr, ei + ti))
        high.append((er - tr, ei - ti))
    return low + high


def product(x, high, low):
    xh = x.astype(BF16)
    xl = (x - xh.astype(F32)).astype(BF16)
    h = high[...]
    total = jnp.dot(xl, h, preferred_element_type=F32)
    total = total + jnp.dot(xh, low[...], preferred_element_type=F32)
    return total + jnp.dot(xh, h, preferred_element_type=F32)


def slot_of(shape):
    lane = lax.broadcasted_iota(jnp.int32, shape, 1)
    return jnp.right_shift(lane + RIM, 4) & (SLOT_COUNT - 1)


def turned(x, by):
    by = by % COLS
    return x if by == 0 else pltpu.roll(x, by, 1)


def filter_body(rims, rows, high, low, high_t, low_t, twiddle, weights, out, wide, spec, flat):
    def load(p):
        x = rows[p].astype(F32)
        return x[:8], x[8:]

    for b, (ur, ui) in enumerate(fft(load, 0, 1, BLOCKS, -1)):
        c, s = twiddle[0, b : b + 1, :], twiddle[1, b : b + 1, :]
        wide[8 * b : 8 * b + 8, :COLS] = ur * c + ui * s
        wide[8 * b : 8 * b + 8, COLS:] = ui * c - ur * s
    spec[...] = product(wide[...], high, low)
    for b in range(BLOCKS):
        spec[8 * b : 8 * b + 8, :] = spec[8 * b : 8 * b + 8, :] * weights[b : b + 1, :]
    wide[...] = product(spec[...], high_t, low_t)

    def load_back(b):
        c, s = twiddle[0, b : b + 1, :], twiddle[1, b : b + 1, :]
        yr, yi = wide[8 * b : 8 * b + 8, :COLS], wide[8 * b : 8 * b + 8, COLS:]
        return yr * c - yi * s, yr * s + yi * c

    blocks = fft(load_back, 0, 1, BLOCKS, 1)
    if not rims:
        for p, (yr, yi) in enumerate(blocks):
            out[p] = jnp.concatenate([yr, yi], axis=0).astype(BF16)
        return
    for p, (yr, yi) in enumerate(blocks):
        for place in {p + 1, 0 if p == BLOCKS - 1 else p + 1, BLOCKS + 1 if p == 0 else p + 1}:
            flat[SLOTS * place : SLOTS * place + 8, :] = yr
            flat[SLOTS * place + 8 : SLOTS * place + 16, :] = yi
    slot = slot_of((BLOCKS, COLS))
    right = (lax.broadcasted_iota(jnp.int32, (BLOCKS, COLS), 1) & 15) < RIM
    first = jnp.zeros((BLOCKS, COLS), F32)
    second = jnp.zeros((BLOCKS, COLS), F32)
    for m in range(MEM):
        before = flat[pl.ds(m, BLOCKS, stride=SLOTS), :]
        after = flat[pl.ds(m + 2 * SLOTS, BLOCKS, stride=SLOTS), :]
        if m < SLOT_COUNT:
            rim = jnp.where(right, turned(after, 16 * m), turned(before, 16 * m))
            first = jnp.where(slot == m, rim, first)
        else:
            for v in range(3):
                q = EXTRA * v + m - SLOT_COUNT
                rim = jnp.where(right, turned(after, 16 * q), turned(before, 16 * q))
                second = jnp.where(slot == q, rim, second)
    flat[pl.ds(SLOTS + MEM, BLOCKS, stride=SLOTS), :] = first
    flat[pl.ds(SLOTS + MEM + 1, BLOCKS, stride=SLOTS), :] = second
    for p in range(BLOCKS):
        out[p] = flat[SLOTS * (p + 1) : SLOTS * (p + 2), :].astype(BF16)


def localize(rows, weights, rims):
    return call(
        functools.partial(filter_body, rims),
        jax.ShapeDtypeStruct((BLOCKS, SLOTS, COLS), BF16),
        [
            VMEM((8 * BLOCKS, 2 * COLS), F32),
            VMEM((8 * BLOCKS, COLS), F32),
            VMEM((SLOTS * (BLOCKS + 2), COLS), F32),
        ],
        7,
    )(rows, *tables(), weights)


def by_row(flat, out):
    for y in range(ROWS):
        x = flat[pl.ds(y, MEM, stride=ROWS), :]
        x = jnp.concatenate([x, jnp.zeros((SLOTS - MEM, COLS), F32)], axis=0)
        out[y] = x.astype(BF16)


def to_send(alpha):
    return call(by_row, jax.ShapeDtypeStruct((ROWS, SLOTS, COLS), BF16))(
        alpha.reshape(MEM * ROWS, COLS)
    )


def contract(ensemble, arrived, from_low, from_high, tiles, out, flat):
    own = lax.axis_index("grp")
    unspread = math.sqrt(MEM * GROUPS - 1)
    flat[...] = arrived[...].astype(F32).reshape(ROWS * SLOTS, COLS)
    totals = [jnp.zeros((ROWS, COLS), F32)] * 3
    for m in range(MEM):
        field = flat[pl.ds(m, ROWS, stride=SLOTS), :]
        for v in range(3):
            totals[v] = totals[v] + ensemble[m, v].astype(F32) * field
    right = (lax.broadcasted_iota(jnp.int32, (16, COLS), 1) & 15) < RIM

    def rim(at, count):
        return jnp.concatenate(
            [
                jnp.where(
                    right,
                    from_high[at + i : at + i + 16, :].astype(F32),
                    from_low[at + i : at + i + 16, :].astype(F32),
                )
                for i in range(0, count, 16)
            ],
            axis=0,
        )

    slot = slot_of((ROWS, COLS))
    first = flat[pl.ds(MEM, ROWS, stride=SLOTS), :]
    second = flat[pl.ds(MEM + 1, ROWS, stride=SLOTS), :]
    extra = rim(3 * ROWS, ROWS) * second
    side = jnp.zeros((ROWS, COLS), F32)
    for v in range(3):
        t = rim(ROWS * v, ROWS) * first
        t = t + jnp.where(jnp.right_shift(slot, 1) == v, extra, 0.0)
        for by in (64, 32, 16):
            t = t + turned(t, by)
        side = jnp.where(slot == v, t, side)
    obs_rim = rim(4 * ROWS, 16)
    mine = jnp.right_shift(lax.broadcasted_iota(jnp.int32, (ROWS, COLS), 0), 2) == own

    def on_own_rows(tile):
        return jnp.where(mine, unspread * jnp.concatenate([tile] * GROUPS, axis=0), 0.0)

    parts = [
        (totals[v] + on_own_rows(tiles[24 + 4 * v : 28 + 4 * v, :])).astype(BF16)
        for v in range(3)
    ]
    parts.append((side + on_own_rows(obs_rim[4:8])).astype(BF16))
    parts.append(
        jnp.concatenate([tiles[:24, :], obs_rim[:4], jnp.zeros((4, COLS), F32)], axis=0).astype(BF16)
    )
    for i, part in enumerate(parts):
        for g in range(GROUPS):
            out[g, ROWS * i : ROWS * i + ROWS, :] = part


def partial_sums(ensemble, arrived, from_low, from_high, tiles):
    return call(
        contract,
        jax.ShapeDtypeStruct((GROUPS, 5 * ROWS, COLS), BF16),
        [VMEM((ROWS * SLOTS, COLS), F32)],
        5,
    )(ensemble, arrived, from_low, from_high, tiles)


def observe(cell, step, innovation, weight, std, control, ensemble, tiles, edges):
    where_row = jnp.right_shift(cell[...], 12) & (TILE_ROWS - 1)
    key = step[...] * TILE_ROWS + where_row
    column = cell[...] & (COLS - 1)
    w = weight[...]
    wd = w * innovation[...]
    n = 3 * TILE_ROWS
    count = w.shape[1]
    mine = lax.broadcasted_iota(jnp.int32, (n, count), 0) == key
    values = jnp.concatenate([jnp.where(mine, w, 0.0), jnp.where(mine, wd, 0.0)], axis=0)
    high = values.astype(BF16)
    rest = values - high.astype(F32)
    mid = rest.astype(BF16)
    low = (rest - mid.astype(F32)).astype(BF16)
    hot = (lax.broadcasted_iota(jnp.int32, (COLS, count), 0) == column).astype(F32).astype(BF16)
    total = jnp.zeros((2 * n, COLS), F32)
    for piece in (low, mid, high):
        total = total + lax.dot_general(
            piece, hot, (((1,), (1,)), ((), ())), preferred_element_type=F32
        )
    static = [std[v] * control[v] for v in range(3)]
    tiles[:24, :] = total
    for v in range(3):
        tiles[24 + 4 * v : 28 + 4 * v, :] = static[v]
    slot = slot_of((ROWS, COLS))
    extra = jnp.zeros((ROWS, COLS), F32)
    for v in range(3):
        packed = jnp.zeros((ROWS, COLS), F32)
        for m in range(SLOT_COUNT):
            packed = jnp.where(slot == m, turned(ensemble[m, v].astype(F32), 16 * m), packed)
        edges[ROWS * v : ROWS * v + ROWS, :] = packed.astype(BF16)
        for m in range(SLOT_COUNT, MEM):
            q = EXTRA * v + m - SLOT_COUNT
            extra = jnp.where(slot == q, turned(ensemble[m, v].astype(F32), 16 * q), extra)
    edges[3 * ROWS : 4 * ROWS, :] = extra.astype(BF16)
    slot = slot_of((TILE_ROWS, COLS))
    sums = jnp.zeros((TILE_ROWS, COLS), F32)
    for f in range(6):
        sums = jnp.where(slot == f, turned(total[4 * f : 4 * f + 4], 16 * f), sums)
    product_rim = jnp.zeros((TILE_ROWS, COLS), F32)
    for v in range(3):
        product_rim = jnp.where(slot == v, turned(static[v], 16 * v), product_rim)
    pad = jnp.zeros((8, COLS), F32)
    edges[4 * ROWS :, :] = jnp.concatenate([sums, product_rim, pad], axis=0).astype(BF16)


def tile_fields(cell, step, innovation, weight, std, control, ensemble):
    flat = [a.reshape(1, -1) for a in (cell, step, innovation, weight)]
    return call(
        observe,
        [
            jax.ShapeDtypeStruct((36, COLS), F32),
            jax.ShapeDtypeStruct((4 * ROWS + 16, COLS), BF16),
        ],
        (),
        7,
    )(*flat, std, control, ensemble)


def window(arrived, ensemble, sent, adj, flat, sums):
    spread = 1.0 / math.sqrt(MEM * GROUPS - 1)
    parts = []
    for i in range(4):
        total = arrived[0, ROWS * i : ROWS * i + ROWS, :].astype(F32)
        for g in range(1, GROUPS):
            total = total + arrived[g, ROWS * i : ROWS * i + ROWS, :].astype(F32)
        parts.append(spread * total)
    for g in range(GROUPS):
        x = arrived[g, 4 * ROWS : 5 * ROWS, :].astype(F32)
        for f in range(7):
            sums[f, TILE_ROWS * g : TILE_ROWS * g + TILE_ROWS, :] = x[4 * f : 4 * f + 4]
    lane = lax.broadcasted_iota(jnp.int32, (ROWS, COLS), 1)
    used = jnp.logical_or(lane < RIM, lane >= COLS - RIM)

    def wide(main, packed, place):
        rim = jnp.where(used, turned(packed, -16 * place), 0.0)
        return jnp.concatenate([main, rim], axis=1)

    row = lax.broadcasted_iota(jnp.int32, (ROWS, 2 * COLS), 0)
    rotation = 0.1 + 0.2 * (row.astype(F32) + 0.5) / ROWS
    down = row < ROWS - 1
    up = row > 0
    half_c = 0.5 * COURANT

    def dx(q):
        return half_c * (pltpu.roll(q, 2 * COLS - 1, 1) - pltpu.roll(q, 1, 1))

    def dy(q):
        below = jnp.where(down, pltpu.roll(q, ROWS - 1, 0), 0.0)
        above = jnp.where(up, pltpu.roll(q, 1, 0), 0.0)
        return half_c * (below - above)

    def forward(h, u, w):
        h1 = h - (dx(u) + dy(w))
        return h1, u - dx(h1) + rotation * w, w - dy(h1) - rotation * u

    def backward(bh, bu, bw):
        a = bh + (dx(bu) + dy(bw))
        return a, bu - rotation * bw + dx(a), bw + rotation * bu + dy(a)

    state = tuple(wide(parts[v], parts[3], v) for v in range(3))
    forcing = []
    for t in range(3):
        w_t = wide(sums[t], sums[6], t)
        v_t = wide(sums[3 + t], sums[6], 3 + t)
        forcing.append(w_t * state[0] - v_t)
        if t < 2:
            state = forward(*state)
    zero = jnp.zeros((ROWS, 2 * COLS), F32)
    bh, bu, bw = backward(forcing[2], zero, zero)
    bh, bu, bw = backward(bh + forcing[1], bu, bw)
    bh = bh + forcing[0]
    fin = [x[:, :COLS] for x in (bh, bu, bw)]
    for v in range(3):
        adj[v] = fin[v]
    for m in range(MEM):
        total = ensemble[m, 0].astype(F32) * fin[0]
        for v in range(1, 3):
            total = total + ensemble[m, v].astype(F32) * fin[v]
        flat[ROWS * m : ROWS * m + ROWS, :] = total
    by_row(flat, sent)


def assimilate(arrived, ensemble):
    return call(
        window,
        [
            jax.ShapeDtypeStruct((ROWS, SLOTS, COLS), BF16),
            jax.ShapeDtypeStruct((3, ROWS, COLS), F32),
        ],
        [VMEM((MEM * ROWS, COLS), F32), VMEM((7, ROWS, COLS), F32)],
        2,
    )(arrived, ensemble)


def add_alpha(alpha, arrived, out, flat):
    spread = 1.0 / math.sqrt(MEM * GROUPS - 1)
    flat[...] = arrived[...].astype(F32).reshape(ROWS * SLOTS, COLS)
    for m in range(MEM):
        out[m] = alpha[m] + spread * flat[pl.ds(m, ROWS, stride=SLOTS), :]


def finish(alpha, arrived):
    return call(
        add_alpha,
        jax.ShapeDtypeStruct((MEM, ROWS, COLS), F32),
        [VMEM((ROWS * SLOTS, COLS), F32)],
        2,
    )(alpha, arrived)


def wave_weights(loc_spectrum):
    side = KEEP // BLOCKS
    first = jnp.arange(KEEP) == 0
    up = jnp.where(first, loc_spectrum, 0.5 * loc_spectrum).reshape(side, BLOCKS)
    after = jnp.concatenate([0.5 * loc_spectrum[1:], jnp.zeros((1,), F32)])
    down = after.reshape(side, BLOCKS)[:, ::-1]
    both = jnp.concatenate([up, down], axis=0).T
    return jnp.concatenate([both, both], axis=1)


def swap(x, axis):
    return lax.all_to_all(x, axis, split_axis=0, concat_axis=0, tiled=True)


def neighbours(x):
    ahead = [(i, (i + 1) % BLOCKS) for i in range(BLOCKS)]
    back = [(t, s) for s, t in ahead]
    return lax.ppermute(x, SP, ahead), lax.ppermute(x, SP, back)


def per_device(
    alpha, ensemble, static_std, control, loc_spectrum, obs_cell, obs_step, innovation, obs_weight
):
    first_row = lax.axis_index("grp") * TILE_ROWS
    rows = swap(to_send(alpha), SP)
    tiles, edges = tile_fields(
        obs_cell, obs_step, innovation, obs_weight, static_std, control, ensemble
    )
    from_low, from_high = neighbours(edges)
    weights = wave_weights(loc_spectrum)
    localized = swap(localize(rows, weights, True), SP)
    summed = swap(partial_sums(ensemble, localized, from_low, from_high, tiles), "grp")
    sent, adjoint = assimilate(summed, ensemble)
    weighted = swap(sent, SP)
    mine = lax.dynamic_slice_in_dim(adjoint, first_row, TILE_ROWS, axis=1)
    grad_control = control + static_std * mine
    filtered = swap(localize(weighted, weights, False), SP)
    return finish(alpha, filtered), grad_control


def solution(mesh):
    torus = Mesh(mesh.devices.reshape(mesh.shape["grp"], 4, 4, 2), GRP_SP)
    placed = (
        P("grp", None, SP),
        P("grp", None, None, SP),
        P(None, "grp", SP),
        P(None, "grp", SP),
        P(),
        P(GRP_SP),
        P(GRP_SP),
        P(GRP_SP),
        P(GRP_SP),
    )
    return jax.shard_map(
        per_device,
        mesh=torus,
        in_specs=placed,
        out_specs=(P("grp", None, SP), P(None, "grp", SP)),
        check_vma=False,
    )
```

```python
import functools
import math

import jax
import jax.numpy as jnp
import numpy as np
from jax import lax
from jax.experimental import pallas as pl
from jax.experimental.pallas import tpu as pltpu
from jax.sharding import Mesh
from jax.sharding import PartitionSpec as P

GRP_SP = ("grp", "sp_0", "sp_1", "sp_2")
SP = ("sp_0", "sp_1", "sp_2")

MEM = 10
SLOTS = 16
ROWS = 32
COLS = 128
BLOCKS = 32
GROUPS = 8
TILE_ROWS = 4
NX = BLOCKS * COLS
KEEP = 1024
ALPHAS = 2 * KEEP // BLOCKS
RIM = 8
SLOT_COUNT = COLS // 16
EXTRA = MEM - SLOT_COUNT
COURANT = 0.4

F32 = jnp.float32
BF16 = jnp.bfloat16
VMEM = pltpu.VMEM


def call(body, out_shape, scratch=(), n_in=1):
    single = not isinstance(out_shape, (list, tuple))
    spec = pl.BlockSpec(memory_space=VMEM)
    return pl.pallas_call(
        body,
        out_shape=out_shape,
        in_specs=[spec] * n_in,
        out_specs=spec if single else [spec] * len(out_shape),
        scratch_shapes=list(scratch),
        compiler_params=pltpu.CompilerParams(vmem_limit_bytes=32 << 20),
    )


def split(table):
    high = table.astype(jnp.bfloat16)
    low = (table - np.asarray(high).astype(np.float64)).astype(jnp.bfloat16)
    return np.asarray(high), np.asarray(low)


def tables():
    j = np.arange(COLS)
    wave = np.concatenate([np.arange(ALPHAS // 2), -1 - np.arange(ALPHAS // 2)])
    angle = 2.0 * np.pi * ((j[:, None] * wave[None, :]) % COLS) / COLS
    c, s = np.cos(angle), np.sin(angle)
    basis = np.concatenate(
        [np.concatenate([c, -s], axis=1), np.concatenate([s, c], axis=1)], axis=0
    )
    turn = 2.0 * np.pi * np.arange(BLOCKS)[:, None] * j[None, :] / NX
    twiddle = np.stack([np.cos(turn), np.sin(turn)]).astype(np.float32)
    high, low = split(basis)
    return high, low, np.ascontiguousarray(high.T), np.ascontiguousarray(low.T), twiddle


def fft(load, start, step, n, sign):
    if n == 1:
        return [load(start)]
    even = fft(load, start, 2 * step, n // 2, sign)
    odd = fft(load, start + step, 2 * step, n // 2, sign)
    low, high = [], []
    for k in range(n // 2):
        er, ei = even[k]
        xr, xi = odd[k]
        if k == 0:
            tr, ti = xr, xi
        elif 4 * k == n:
            tr, ti = (-xi, xr) if sign > 0 else (xi, -xr)
        elif 8 * k == n:
            r = math.sqrt(0.5)
            tr, ti = ((xr - xi) * r, (xr + xi) * r) if sign > 0 else ((xr + xi) * r, (xi - xr) * r)
        elif 8 * k == 3 * n:
            r = math.sqrt(0.5)
            tr, ti = (-(xr + xi) * r, (xr - xi) * r) if sign > 0 else ((xi - xr) * r, -(xr + xi) * r)
        else:
            c = math.cos(2.0 * math.pi * k / n)
            s = sign * math.sin(2.0 * math.pi * k / n)
            tr, ti = xr * c - xi * s, xr * s + xi * c
        low.append((er + tr, ei + ti))
        high.append((er - tr, ei - ti))
    return low + high


def product(x, high, low):
    xh = x.astype(BF16)
    xl = (x - xh.astype(F32)).astype(BF16)
    h = high[...]
    total = jnp.dot(xl, h, preferred_element_type=F32)
    total = total + jnp.dot(xh, low[...], preferred_element_type=F32)
    return total + jnp.dot(xh, h, preferred_element_type=F32)


def slot_of(shape):
    lane = lax.broadcasted_iota(jnp.int32, shape, 1)
    return jnp.right_shift(lane + RIM, 4) & (SLOT_COUNT - 1)


def turned(x, by):
    by = by % COLS
    return x if by == 0 else pltpu.roll(x, by, 1)


def pack_slots(field, count):
    slot = slot_of((count, COLS))
    first = jnp.zeros((count, COLS), F32)
    for m in range(SLOT_COUNT):
        first = jnp.where(slot == m, turned(field(m), 16 * m), first)
    return first


def pack_extra(field, count):
    slot = slot_of((count, COLS))
    extra = jnp.zeros((count, COLS), F32)
    for v in range(3):
        for i in range(EXTRA):
            q = EXTRA * v + i
            extra = jnp.where(slot == q, turned(field(SLOT_COUNT + i, v), 16 * q), extra)
    return extra


def filter_body(rims, *refs):
    rows, high, low, high_t, low_t, twiddle, weights = refs[:7]
    if rims:
        edges, out, wide, spec, flat, arrived = refs[7:]
    else:
        out, wide, spec = refs[7:]

    def load(p):
        x = rows[p].astype(F32)
        return x[:8], x[8:]

    for b, (ur, ui) in enumerate(fft(load, 0, 1, BLOCKS, -1)):
        c, s = twiddle[0, b : b + 1, :], twiddle[1, b : b + 1, :]
        wide[8 * b : 8 * b + 8, :COLS] = ur * c + ui * s
        wide[8 * b : 8 * b + 8, COLS:] = ui * c - ur * s
    spec[...] = product(wide[...], high, low)
    for b in range(BLOCKS):
        spec[8 * b : 8 * b + 8, :] = spec[8 * b : 8 * b + 8, :] * weights[b : b + 1, :]
    wide[...] = product(spec[...], high_t, low_t)

    def load_back(b):
        c, s = twiddle[0, b : b + 1, :], twiddle[1, b : b + 1, :]
        yr, yi = wide[8 * b : 8 * b + 8, :COLS], wide[8 * b : 8 * b + 8, COLS:]
        return yr * c - yi * s, yr * s + yi * c

    blocks = fft(load_back, 0, 1, BLOCKS, 1)
    if not rims:
        for p, (yr, yi) in enumerate(blocks):
            out[p] = jnp.concatenate([yr, yi], axis=0).astype(BF16)
        return
    arrived[...] = rows[...].astype(F32).reshape(BLOCKS * SLOTS, COLS)
    for p, (yr, yi) in enumerate(blocks):
        flat[SLOTS * p : SLOTS * p + 8, :] = yr
        flat[SLOTS * p + 8 : SLOTS * p + 16, :] = yi

    def every(source, place):
        return source[pl.ds(place, BLOCKS, stride=SLOTS), :]

    first = pack_slots(lambda m: every(flat, m), BLOCKS)
    extra = pack_extra(lambda m, v: every(flat, m), BLOCKS)
    extra = extra * every(arrived, MEM + 3)
    slot = slot_of((BLOCKS, COLS))
    right = (lax.broadcasted_iota(jnp.int32, (BLOCKS, COLS), 1) & 15) < RIM
    side = jnp.zeros((BLOCKS, COLS), F32)
    for v in range(3):
        t = first * every(arrived, MEM + v)
        t = t + jnp.where(jnp.right_shift(slot, 1) == v, extra, 0.0)
        for by in (64, 32, 16):
            t = t + turned(t, by)
        side = jnp.where(slot == v, t, side)
    side = jnp.where(right, pltpu.roll(side, BLOCKS - 1, 0), pltpu.roll(side, 1, 0))
    flat[pl.ds(MEM, BLOCKS, stride=SLOTS), :] = side
    own_edges = edges[:5, :]
    for p in range(BLOCKS):
        flat[SLOTS * p + MEM + 1 : SLOTS * p + SLOTS, :] = own_edges
        out[p] = flat[SLOTS * p : SLOTS * p + SLOTS, :].astype(BF16)


def localize(rows, weights, edges=None):
    rims = edges is not None
    scratch = [VMEM((8 * BLOCKS, 2 * COLS), F32), VMEM((8 * BLOCKS, COLS), F32)]
    if rims:
        scratch += [VMEM((SLOTS * BLOCKS, COLS), F32)] * 2
    return call(
        functools.partial(filter_body, rims),
        jax.ShapeDtypeStruct((BLOCKS, SLOTS, COLS), BF16),
        scratch,
        8 if rims else 7,
    )(rows, *tables(), weights, *([edges] if rims else []))


def by_row(flat, out):
    for y in range(ROWS):
        x = flat[pl.ds(y, MEM, stride=ROWS), :]
        x = jnp.concatenate([x, jnp.zeros((SLOTS - MEM, COLS), F32)], axis=0)
        out[y] = x.astype(BF16)


def send_body(alpha, ensemble, out, flat):
    for m in range(MEM):
        flat[pl.ds(m, ROWS, stride=SLOTS), :] = alpha[m]
    for v in range(3):
        flat[pl.ds(MEM + v, ROWS, stride=SLOTS), :] = pack_slots(
            lambda m: ensemble[m, v].astype(F32), ROWS
        )
    flat[pl.ds(MEM + 3, ROWS, stride=SLOTS), :] = pack_extra(
        lambda m, v: ensemble[m, v].astype(F32), ROWS
    )
    for place in range(MEM + 4, SLOTS):
        flat[pl.ds(place, ROWS, stride=SLOTS), :] = jnp.zeros((ROWS, COLS), F32)
    out[...] = flat[...].reshape(ROWS, SLOTS, COLS).astype(BF16)


def to_send(alpha, ensemble):
    return call(
        send_body,
        jax.ShapeDtypeStruct((ROWS, SLOTS, COLS), BF16),
        [VMEM((ROWS * SLOTS, COLS), F32)],
        2,
    )(alpha, ensemble)


def contract(ensemble, arrived, tiles, out, flat):
    own = lax.axis_index("grp")
    column = lax.axis_index(SP)
    unspread = math.sqrt(MEM * GROUPS - 1)
    flat[...] = arrived[...].astype(F32).reshape(ROWS * SLOTS, COLS)
    totals = [jnp.zeros((ROWS, COLS), F32)] * 3
    for m in range(MEM):
        field = flat[pl.ds(m, ROWS, stride=SLOTS), :]
        for v in range(3):
            totals[v] = totals[v] + ensemble[m, v].astype(F32) * field
    side = flat[pl.ds(MEM, ROWS, stride=SLOTS), :]
    right = (lax.broadcasted_iota(jnp.int32, (SLOTS, COLS), 1) & 15) < RIM
    after = arrived[(column + 1) & (BLOCKS - 1)].astype(F32)
    before = arrived[(column + BLOCKS - 1) & (BLOCKS - 1)].astype(F32)
    rim = jnp.where(right, after, before)
    obs_rim = rim[MEM + 1 : MEM + 5]
    last = rim[MEM + 5 : MEM + 6]
    slot = slot_of((TILE_ROWS, COLS))
    static_rim = jnp.where(
        slot == 2,
        jnp.concatenate([turned(last, 16 * (2 - r)) for r in range(TILE_ROWS)], axis=0),
        turned(obs_rim, 32),
    )
    mine = jnp.right_shift(lax.broadcasted_iota(jnp.int32, (ROWS, COLS), 0), 2) == own

    def on_own_rows(tile):
        return jnp.where(mine, unspread * jnp.concatenate([tile] * GROUPS, axis=0), 0.0)

    parts = [
        (totals[v] + on_own_rows(tiles[24 + 4 * v : 28 + 4 * v, :])).astype(BF16)
        for v in range(3)
    ]
    parts.append((side + on_own_rows(static_rim)).astype(BF16))
    parts.append(
        jnp.concatenate([tiles[:24, :], obs_rim, jnp.zeros((4, COLS), F32)], axis=0).astype(BF16)
    )
    for i, part in enumerate(parts):
        for g in range(GROUPS):
            out[g, ROWS * i : ROWS * i + ROWS, :] = part


def partial_sums(ensemble, arrived, tiles):
    return call(
        contract,
        jax.ShapeDtypeStruct((GROUPS, 5 * ROWS, COLS), BF16),
        [VMEM((ROWS * SLOTS, COLS), F32)],
        3,
    )(ensemble, arrived, tiles)


def observe(cell, step, innovation, weight, std, control, tiles, edges):
    where_row = jnp.right_shift(cell[...], 12) & (TILE_ROWS - 1)
    key = step[...] * TILE_ROWS + where_row
    column = cell[...] & (COLS - 1)
    w = weight[...]
    wd = w * innovation[...]
    n = 3 * TILE_ROWS
    count = w.shape[1]
    mine = lax.broadcasted_iota(jnp.int32, (n, count), 0) == key
    values = jnp.concatenate([jnp.where(mine, w, 0.0), jnp.where(mine, wd, 0.0)], axis=0)
    high = values.astype(BF16)
    rest = values - high.astype(F32)
    mid = rest.astype(BF16)
    low = (rest - mid.astype(F32)).astype(BF16)
    hot = (lax.broadcasted_iota(jnp.int32, (COLS, count), 0) == column).astype(F32).astype(BF16)
    total = jnp.zeros((2 * n, COLS), F32)
    for piece in (low, mid, high):
        total = total + lax.dot_general(
            piece, hot, (((1,), (1,)), ((), ())), preferred_element_type=F32
        )
    static = [std[v] * control[v] for v in range(3)]
    tiles[:24, :] = total
    for v in range(3):
        tiles[24 + 4 * v : 28 + 4 * v, :] = static[v]
    slot = slot_of((TILE_ROWS, COLS))
    sums = jnp.zeros((TILE_ROWS, COLS), F32)
    for f in range(6):
        sums = jnp.where(slot == f, turned(total[4 * f : 4 * f + 4], 16 * f), sums)
    for v in range(2):
        sums = jnp.where(slot == 6 + v, turned(static[v], 16 * (6 + v)), sums)
    slot = slot_of((1, COLS))
    last = jnp.zeros((1, COLS), F32)
    for r in range(TILE_ROWS):
        last = jnp.where(slot == r, turned(static[2][r : r + 1], 16 * r), last)
    edges[...] = jnp.concatenate([sums, last, jnp.zeros((3, COLS), F32)], axis=0)


def tile_fields(cell, step, innovation, weight, std, control):
    flat = [a.reshape(1, -1) for a in (cell, step, innovation, weight)]
    return call(
        observe,
        [jax.ShapeDtypeStruct((36, COLS), F32), jax.ShapeDtypeStruct((8, COLS), F32)],
        (),
        6,
    )(*flat, std, control)


def window(arrived, ensemble, sent, tile, flat, sums):
    own = lax.axis_index("grp")
    spread = 1.0 / math.sqrt(MEM * GROUPS - 1)
    parts = []
    for i in range(4):
        total = arrived[0, ROWS * i : ROWS * i + ROWS, :].astype(F32)
        for g in range(1, GROUPS):
            total = total + arrived[g, ROWS * i : ROWS * i + ROWS, :].astype(F32)
        parts.append(spread * total)
    for g in range(GROUPS):
        x = arrived[g, 4 * ROWS : 5 * ROWS, :].astype(F32)
        for f in range(7):
            sums[f, TILE_ROWS * g : TILE_ROWS * g + TILE_ROWS, :] = x[4 * f : 4 * f + 4]
    lane = lax.broadcasted_iota(jnp.int32, (ROWS, COLS), 1)
    used = jnp.logical_or(lane < RIM, lane >= COLS - RIM)

    def wide(main, packed, place):
        rim = jnp.where(used, turned(packed, -16 * place), 0.0)
        return jnp.concatenate([main, rim], axis=1)

    row = lax.broadcasted_iota(jnp.int32, (ROWS, 2 * COLS), 0)
    rotation = 0.1 + 0.2 * (row.astype(F32) + 0.5) / ROWS
    down = row < ROWS - 1
    up = row > 0
    half_c = 0.5 * COURANT

    def dx(q):
        return half_c * (pltpu.roll(q, 2 * COLS - 1, 1) - pltpu.roll(q, 1, 1))

    def dy(q):
        below = jnp.where(down, pltpu.roll(q, ROWS - 1, 0), 0.0)
        above = jnp.where(up, pltpu.roll(q, 1, 0), 0.0)
        return half_c * (below - above)

    def forward(h, u, w):
        h1 = h - (dx(u) + dy(w))
        return h1, u - dx(h1) + rotation * w, w - dy(h1) - rotation * u

    def backward(bh, bu, bw):
        a = bh + (dx(bu) + dy(bw))
        return a, bu - rotation * bw + dx(a), bw + rotation * bu + dy(a)

    state = tuple(wide(parts[v], parts[3], v) for v in range(3))
    forcing = []
    for t in range(3):
        w_t = wide(sums[t], sums[6], t)
        v_t = wide(sums[3 + t], sums[6], 3 + t)
        forcing.append(w_t * state[0] - v_t)
        if t < 2:
            state = forward(*state)
    zero = jnp.zeros((ROWS, 2 * COLS), F32)
    bh, bu, bw = backward(forcing[2], zero, zero)
    bh, bu, bw = backward(bh + forcing[1], bu, bw)
    bh = bh + forcing[0]
    fin = [x[:, :COLS] for x in (bh, bu, bw)]
    for v in range(3):
        mine = fin[v][:TILE_ROWS]
        for g in range(1, GROUPS):
            mine = jnp.where(own == g, fin[v][TILE_ROWS * g : TILE_ROWS * g + TILE_ROWS], mine)
        tile[v] = mine
    for m in range(MEM):
        total = ensemble[m, 0].astype(F32) * fin[0]
        for v in range(1, 3):
            total = total + ensemble[m, v].astype(F32) * fin[v]
        flat[ROWS * m : ROWS * m + ROWS, :] = total
    by_row(flat, sent)


def assimilate(arrived, ensemble):
    return call(
        window,
        [
            jax.ShapeDtypeStruct((ROWS, SLOTS, COLS), BF16),
            jax.ShapeDtypeStruct((3, TILE_ROWS, COLS), F32),
        ],
        [VMEM((MEM * ROWS, COLS), F32), VMEM((7, ROWS, COLS), F32)],
        2,
    )(arrived, ensemble)


def add_alpha(alpha, arrived, tile, std, control, out, grad, flat):
    spread = 1.0 / math.sqrt(MEM * GROUPS - 1)
    for v in range(3):
        grad[v] = control[v] + std[v] * tile[v]
    flat[...] = arrived[...].astype(F32).reshape(ROWS * SLOTS, COLS)
    for m in range(MEM):
        out[m] = alpha[m] + spread * flat[pl.ds(m, ROWS, stride=SLOTS), :]


def finish(alpha, arrived, tile, std, control):
    return call(
        add_alpha,
        [
            jax.ShapeDtypeStruct((MEM, ROWS, COLS), F32),
            jax.ShapeDtypeStruct((3, TILE_ROWS, COLS), F32),
        ],
        [VMEM((ROWS * SLOTS, COLS), F32)],
        5,
    )(alpha, arrived, tile, std, control)


def wave_weights(loc_spectrum):
    side = KEEP // BLOCKS
    first = jnp.arange(KEEP) == 0
    up = jnp.where(first, loc_spectrum, 0.5 * loc_spectrum).reshape(side, BLOCKS)
    after = jnp.concatenate([0.5 * loc_spectrum[1:], jnp.zeros((1,), F32)])
    down = after.reshape(side, BLOCKS)[:, ::-1]
    both = jnp.concatenate([up, down], axis=0).T
    return jnp.concatenate([both, both], axis=1)


def swap(x, axis):
    return lax.all_to_all(x, axis, split_axis=0, concat_axis=0, tiled=True)


def per_device(
    alpha, ensemble, static_std, control, loc_spectrum, obs_cell, obs_step, innovation, obs_weight
):
    rows = swap(to_send(alpha, ensemble), SP)
    tiles, edges = tile_fields(
        obs_cell, obs_step, innovation, obs_weight, static_std, control
    )
    weights = wave_weights(loc_spectrum)
    localized = swap(localize(rows, weights, edges), SP)
    summed = swap(partial_sums(ensemble, localized, tiles), "grp")
    sent, tile = assimilate(summed, ensemble)
    filtered = swap(localize(swap(sent, SP), weights), SP)
    return finish(alpha, filtered, tile, static_std, control)


def solution(mesh):
    torus = Mesh(mesh.devices.reshape(mesh.shape["grp"], 4, 4, 2), GRP_SP)
    placed = (
        P("grp", None, SP),
        P("grp", None, None, SP),
        P(None, "grp", SP),
        P(None, "grp", SP),
        P(),
        P(GRP_SP),
        P(GRP_SP),
        P(GRP_SP),
        P(GRP_SP),
    )
    return jax.shard_map(
        per_device,
        mesh=torus,
        in_specs=placed,
        out_specs=(P("grp", None, SP), P(None, "grp", SP)),
        check_vma=False,
    )
```

```python
import functools
import math

import jax
import jax.numpy as jnp
import numpy as np
from jax import lax
from jax.experimental import pallas as pl
from jax.experimental.pallas import tpu as pltpu
from jax.sharding import PartitionSpec as P

SP = "sp"

MEM = 10
SLOTS = 16
ROWS = 32
COLS = 128
BLOCKS = 32
GROUPS = 8
TILE_ROWS = 4
NX = BLOCKS * COLS
KEEP = 1024
ALPHAS = 2 * KEEP // BLOCKS
RIM = 8
SLOT_COUNT = COLS // 16
EXTRA = MEM - SLOT_COUNT
COURANT = 0.4

HEADS = (21, 21, 6, 21, 21)


def places(count, head):
    place = list(range(count))
    place[0], place[head] = head, 0
    return place


FIRST, SECOND, THIRD, FOURTH, FIFTH = (
    places(GROUPS if i == 2 else BLOCKS, head) for i, head in enumerate(HEADS)
)

F32 = jnp.float32
BF16 = jnp.bfloat16
VMEM = pltpu.VMEM


def call(body, out_shape, scratch=(), n_in=1):
    single = not isinstance(out_shape, (list, tuple))
    spec = pl.BlockSpec(memory_space=VMEM)
    return pl.pallas_call(
        body,
        out_shape=out_shape,
        in_specs=[spec] * n_in,
        out_specs=spec if single else [spec] * len(out_shape),
        scratch_shapes=list(scratch),
        compiler_params=pltpu.CompilerParams(vmem_limit_bytes=32 << 20),
    )


def split(table):
    high = table.astype(jnp.bfloat16)
    low = (table - np.asarray(high).astype(np.float64)).astype(jnp.bfloat16)
    return np.asarray(high), np.asarray(low)


def tables():
    j = np.arange(COLS)
    wave = np.concatenate([np.arange(ALPHAS // 2), -1 - np.arange(ALPHAS // 2)])
    angle = 2.0 * np.pi * ((j[:, None] * wave[None, :]) % COLS) / COLS
    c, s = np.cos(angle), np.sin(angle)
    basis = np.concatenate(
        [np.concatenate([c, -s], axis=1), np.concatenate([s, c], axis=1)], axis=0
    )
    turn = 2.0 * np.pi * np.arange(BLOCKS)[:, None] * j[None, :] / NX
    twiddle = np.stack([np.cos(turn), np.sin(turn)]).astype(np.float32)
    high, low = split(basis)
    return high, low, np.ascontiguousarray(high.T), np.ascontiguousarray(low.T), twiddle


def fft(load, start, step, n, sign):
    if n == 1:
        return [load(start)]
    even = fft(load, start, 2 * step, n // 2, sign)
    odd = fft(load, start + step, 2 * step, n // 2, sign)
    low, high = [], []
    for k in range(n // 2):
        er, ei = even[k]
        xr, xi = odd[k]
        if k == 0:
            tr, ti = xr, xi
        elif 4 * k == n:
            tr, ti = (-xi, xr) if sign > 0 else (xi, -xr)
        elif 8 * k == n:
            r = math.sqrt(0.5)
            tr, ti = ((xr - xi) * r, (xr + xi) * r) if sign > 0 else ((xr + xi) * r, (xi - xr) * r)
        elif 8 * k == 3 * n:
            r = math.sqrt(0.5)
            tr, ti = (-(xr + xi) * r, (xr - xi) * r) if sign > 0 else ((xi - xr) * r, -(xr + xi) * r)
        else:
            c = math.cos(2.0 * math.pi * k / n)
            s = sign * math.sin(2.0 * math.pi * k / n)
            tr, ti = xr * c - xi * s, xr * s + xi * c
        low.append((er + tr, ei + ti))
        high.append((er - tr, ei - ti))
    return low + high


def product(x, high, low):
    xh = x.astype(BF16)
    xl = (x - xh.astype(F32)).astype(BF16)
    h = high[...]
    total = jnp.dot(xl, h, preferred_element_type=F32)
    total = total + jnp.dot(xh, low[...], preferred_element_type=F32)
    return total + jnp.dot(xh, h, preferred_element_type=F32)


def slot_of(shape):
    lane = lax.broadcasted_iota(jnp.int32, shape, 1)
    return jnp.right_shift(lane + RIM, 4) & (SLOT_COUNT - 1)


def turned(x, by):
    by = by % COLS
    return x if by == 0 else pltpu.roll(x, by, 1)


def pack_slots(field, count):
    slot = slot_of((count, COLS))
    first = jnp.zeros((count, COLS), F32)
    for m in range(SLOT_COUNT):
        first = jnp.where(slot == m, turned(field(m), 16 * m), first)
    return first


def pack_extra(field, count):
    slot = slot_of((count, COLS))
    extra = jnp.zeros((count, COLS), F32)
    for v in range(3):
        for i in range(EXTRA):
            q = EXTRA * v + i
            extra = jnp.where(slot == q, turned(field(SLOT_COUNT + i, v), 16 * q), extra)
    return extra


def filter_body(rims, come, go, *refs):
    rows, high, low, high_t, low_t, twiddle, weights = refs[:7]
    if rims:
        edges, out, wide, spec, flat, arrived = refs[7:]
    else:
        out, wide, spec = refs[7:]

    def load(p):
        x = rows[come[p]].astype(F32)
        if rims:
            arrived[8 * p : 8 * p + 8, :] = x[8:]
        return x[:8], x[8:]

    for b, (ur, ui) in enumerate(fft(load, 0, 1, BLOCKS, -1)):
        c, s = twiddle[0, b : b + 1, :], twiddle[1, b : b + 1, :]
        wide[8 * b : 8 * b + 8, :COLS] = ur * c + ui * s
        wide[8 * b : 8 * b + 8, COLS:] = ui * c - ur * s
    spec[...] = product(wide[...], high, low)
    for b in range(BLOCKS):
        spec[8 * b : 8 * b + 8, :] = spec[8 * b : 8 * b + 8, :] * weights[b : b + 1, :]
    wide[...] = product(spec[...], high_t, low_t)

    def load_back(b):
        c, s = twiddle[0, b : b + 1, :], twiddle[1, b : b + 1, :]
        yr, yi = wide[8 * b : 8 * b + 8, :COLS], wide[8 * b : 8 * b + 8, COLS:]
        return yr * c - yi * s, yr * s + yi * c

    blocks = fft(load_back, 0, 1, BLOCKS, 1)
    if not rims:
        for p, (yr, yi) in enumerate(blocks):
            out[go[p]] = jnp.concatenate([yr, yi], axis=0).astype(BF16)
        return
    for p, (yr, yi) in enumerate(blocks):
        flat[SLOTS * p : SLOTS * p + 8, :] = yr
        flat[SLOTS * p + 8 : SLOTS * p + 16, :] = yi

    def every(source, place):
        return source[pl.ds(place, BLOCKS, stride=SLOTS), :]

    def edge(i):
        return arrived[pl.ds(MEM - 8 + i, BLOCKS, stride=8), :]

    first = pack_slots(lambda m: every(flat, m), BLOCKS)
    extra = pack_extra(lambda m, v: every(flat, m), BLOCKS)
    extra = extra * edge(3)
    slot = slot_of((BLOCKS, COLS))
    right = (lax.broadcasted_iota(jnp.int32, (BLOCKS, COLS), 1) & 15) < RIM
    side = jnp.zeros((BLOCKS, COLS), F32)
    for v in range(3):
        t = first * edge(v)
        t = t + jnp.where(jnp.right_shift(slot, 1) == v, extra, 0.0)
        for by in (64, 32, 16):
            t = t + turned(t, by)
        side = jnp.where(slot == v, t, side)
    side = jnp.where(right, pltpu.roll(side, BLOCKS - 1, 0), pltpu.roll(side, 1, 0))
    flat[pl.ds(MEM, BLOCKS, stride=SLOTS), :] = side
    own_edges = edges[:5, :]
    for p in range(BLOCKS):
        flat[SLOTS * p + MEM + 1 : SLOTS * p + SLOTS, :] = own_edges
        out[go[p]] = flat[SLOTS * p : SLOTS * p + SLOTS, :].astype(BF16)


def localize(rows, weights, come, go, edges=None):
    rims = edges is not None
    scratch = [VMEM((8 * BLOCKS, 2 * COLS), F32), VMEM((8 * BLOCKS, COLS), F32)]
    if rims:
        scratch += [VMEM((SLOTS * BLOCKS, COLS), F32), VMEM((8 * BLOCKS, COLS), F32)]
    return call(
        functools.partial(filter_body, rims, come, go),
        jax.ShapeDtypeStruct((BLOCKS, SLOTS, COLS), BF16),
        scratch,
        8 if rims else 7,
    )(rows, *tables(), weights, *([edges] if rims else []))


def by_row(flat, out, order):
    for y, place in enumerate(order):
        x = flat[pl.ds(y, MEM, stride=ROWS), :]
        x = jnp.concatenate([x, jnp.zeros((SLOTS - MEM, COLS), F32)], axis=0)
        out[place] = x.astype(BF16)


def pack_weights(loc, out, square, sheet):
    x = loc[...]
    for r in range(4):
        sheet[pl.ds(r, 8, stride=4), :] = turned(x, -BLOCKS * r)
    up = sheet[...]
    lane = lax.broadcasted_iota(jnp.int32, (BLOCKS, COLS), 1)
    row = lax.broadcasted_iota(jnp.int32, (BLOCKS, COLS), 0)
    next_row = jnp.where(row < BLOCKS - 1, pltpu.roll(up, BLOCKS - 1, 0), 0.0)
    down = jnp.where(lane == BLOCKS - 1, turned(next_row, BLOCKS - 1), turned(up, -1))
    both = jnp.concatenate([up, down, jnp.zeros((2 * BLOCKS, COLS), F32)], axis=0)
    square[...] = both.T
    for b in range(BLOCKS):
        sheet[b : b + 1, :] = square[BLOCKS - 1 - b : BLOCKS - b, :]
    h = jnp.where(lane < BLOCKS, square[:BLOCKS, :], jnp.where(lane < 2 * BLOCKS, sheet[...], 0.0))
    h = jnp.where(jnp.logical_and(row == 0, lane == 0), h, 0.5 * h)
    out[...] = h + turned(h, 2 * BLOCKS)


PIECE = 2
SMALL = 7


def first_body(
    alpha, ensemble, loc, cell, step, innovation, weight, std, control,
    out, tiles, edges, weights,
    alpha_v, ens_v, loc_v, cell_v, step_v, innovation_v, weight_v, std_v, control_v,
    flat, square, sheet, small_sem, alpha_sem, ens_sem,
):
    small = [
        pltpu.make_async_copy(a, b, small_sem.at[i])
        for i, (a, b) in enumerate(
            (
                (cell, cell_v),
                (step, step_v),
                (innovation, innovation_v),
                (weight, weight_v),
                (std, std_v),
                (control, control_v),
                (loc, loc_v),
            )
        )
    ]
    count = MEM // PIECE

    def pieces(source, target, sem):
        return [
            pltpu.make_async_copy(
                source.at[pl.ds(PIECE * i, PIECE)], target.at[pl.ds(PIECE * i, PIECE)], sem.at[i]
            )
            for i in range(count)
        ]

    from_alpha = pieces(alpha, alpha_v, alpha_sem)
    from_ensemble = pieces(ensemble, ens_v, ens_sem)
    for copy in small + from_alpha + from_ensemble:
        copy.start()
    for copy in small:
        copy.wait()
    observe(cell_v, step_v, innovation_v, weight_v, std_v, control_v, tiles, edges)
    pack_weights(loc_v, weights, square, sheet)
    for place in range(MEM + 4, SLOTS):
        flat[pl.ds(place, ROWS, stride=SLOTS), :] = jnp.zeros((ROWS, COLS), F32)
    for i, copy in enumerate(from_alpha):
        copy.wait()
        for m in range(PIECE * i, PIECE * i + PIECE):
            flat[pl.ds(m, ROWS, stride=SLOTS), :] = alpha_v[m]
    for copy in from_ensemble:
        copy.wait()
    for v in range(3):
        flat[pl.ds(MEM + v, ROWS, stride=SLOTS), :] = pack_slots(
            lambda m: ens_v[m, v].astype(F32), ROWS
        )
    flat[pl.ds(MEM + 3, ROWS, stride=SLOTS), :] = pack_extra(
        lambda m, v: ens_v[m, v].astype(F32), ROWS
    )
    for y, place in enumerate(FIRST):
        out[place] = flat[SLOTS * y : SLOTS * y + SLOTS, :].astype(BF16)


def first_step(alpha, ensemble, loc, cell, step, innovation, weight, std, control):
    far = pl.BlockSpec(memory_space=pltpu.HBM)
    near = pl.BlockSpec(memory_space=VMEM)
    line = (1, cell.shape[0])
    sems = pltpu.SemaphoreType.DMA
    return pl.pallas_call(
        first_body,
        out_shape=[
            jax.ShapeDtypeStruct((ROWS, SLOTS, COLS), BF16),
            jax.ShapeDtypeStruct((36, COLS), F32),
            jax.ShapeDtypeStruct((8, COLS), F32),
            jax.ShapeDtypeStruct((BLOCKS, COLS), F32),
        ],
        in_specs=[far] * 9,
        out_specs=[near] * 4,
        scratch_shapes=[
            VMEM(alpha.shape, F32),
            VMEM(ensemble.shape, BF16),
            VMEM((8, COLS), F32),
            VMEM(line, jnp.int32),
            VMEM(line, jnp.int32),
            VMEM(line, F32),
            VMEM(line, F32),
            VMEM(std.shape, F32),
            VMEM(control.shape, F32),
            VMEM((ROWS * SLOTS, COLS), F32),
            VMEM((COLS, COLS), F32),
            VMEM((BLOCKS, COLS), F32),
            sems((SMALL,)),
            sems((MEM // PIECE,)),
            sems((MEM // PIECE,)),
        ],
        compiler_params=pltpu.CompilerParams(vmem_limit_bytes=32 << 20),
    )(
        *[
            pltpu.with_memory_space_constraint(a, pltpu.HBM)
            for a in (
                alpha,
                ensemble,
                loc.reshape(8, COLS),
                *[a.reshape(line) for a in (cell, step, innovation, weight)],
                std,
                control,
            )
        ]
    )


def contract(ensemble, arrived, tiles, out, flat):
    own = lax.axis_index("grp")
    column = lax.axis_index(SP)
    unspread = math.sqrt(MEM * GROUPS - 1)
    for y, place in enumerate(SECOND):
        flat[SLOTS * y : SLOTS * y + SLOTS, :] = arrived[place].astype(F32)
    totals = [jnp.zeros((ROWS, COLS), F32)] * 3
    for m in range(MEM):
        field = flat[pl.ds(m, ROWS, stride=SLOTS), :]
        for v in range(3):
            totals[v] = totals[v] + ensemble[m, v].astype(F32) * field
    side = flat[pl.ds(MEM, ROWS, stride=SLOTS), :]
    right = (lax.broadcasted_iota(jnp.int32, (SLOTS, COLS), 1) & 15) < RIM

    def block(y):
        return flat[pl.ds(pl.multiple_of(SLOTS * (y & (BLOCKS - 1)), SLOTS), SLOTS), :]

    after = block(column + 1)
    before = block(column + BLOCKS - 1)
    rim = jnp.where(right, after, before)
    obs_rim = rim[MEM + 1 : MEM + 5]
    last = rim[MEM + 5 : MEM + 6]
    slot = slot_of((TILE_ROWS, COLS))
    static_rim = jnp.where(
        slot == 2,
        jnp.concatenate([turned(last, 16 * (2 - r)) for r in range(TILE_ROWS)], axis=0),
        turned(obs_rim, 32),
    )
    mine = jnp.right_shift(lax.broadcasted_iota(jnp.int32, (ROWS, COLS), 0), 2) == own

    def on_own_rows(tile):
        return jnp.where(mine, unspread * jnp.concatenate([tile] * GROUPS, axis=0), 0.0)

    parts = [
        (totals[v] + on_own_rows(tiles[24 + 4 * v : 28 + 4 * v, :])).astype(BF16)
        for v in range(3)
    ]
    parts.append((side + on_own_rows(static_rim)).astype(BF16))
    parts.append(
        jnp.concatenate([tiles[:24, :], obs_rim, jnp.zeros((4, COLS), F32)], axis=0).astype(BF16)
    )
    for i, part in enumerate(parts):
        for g in range(GROUPS):
            out[g, ROWS * i : ROWS * i + ROWS, :] = part


def partial_sums(ensemble, arrived, tiles):
    return call(
        contract,
        jax.ShapeDtypeStruct((GROUPS, 5 * ROWS, COLS), BF16),
        [VMEM((ROWS * SLOTS, COLS), F32)],
        3,
    )(ensemble, arrived, tiles)


def observe(cell, step, innovation, weight, std, control, tiles, edges):
    where_row = jnp.right_shift(cell[...], 12) & (TILE_ROWS - 1)
    key = step[...] * TILE_ROWS + where_row
    column = cell[...] & (COLS - 1)
    w = weight[...]
    wd = w * innovation[...]
    n = 3 * TILE_ROWS
    count = w.shape[1]
    mine = lax.broadcasted_iota(jnp.int32, (n, count), 0) == key
    values = jnp.concatenate([jnp.where(mine, w, 0.0), jnp.where(mine, wd, 0.0)], axis=0)
    high = values.astype(BF16)
    rest = values - high.astype(F32)
    mid = rest.astype(BF16)
    low = (rest - mid.astype(F32)).astype(BF16)
    hot = (lax.broadcasted_iota(jnp.int32, (COLS, count), 0) == column).astype(F32).astype(BF16)
    total = jnp.zeros((2 * n, COLS), F32)
    for piece in (low, mid, high):
        total = total + lax.dot_general(
            piece, hot, (((1,), (1,)), ((), ())), preferred_element_type=F32
        )
    static = [std[v] * control[v] for v in range(3)]
    tiles[:24, :] = total
    for v in range(3):
        tiles[24 + 4 * v : 28 + 4 * v, :] = static[v]
    slot = slot_of((TILE_ROWS, COLS))
    sums = jnp.zeros((TILE_ROWS, COLS), F32)
    for f in range(6):
        sums = jnp.where(slot == f, turned(total[4 * f : 4 * f + 4], 16 * f), sums)
    for v in range(2):
        sums = jnp.where(slot == 6 + v, turned(static[v], 16 * (6 + v)), sums)
    slot = slot_of((1, COLS))
    last = jnp.zeros((1, COLS), F32)
    for r in range(TILE_ROWS):
        last = jnp.where(slot == r, turned(static[2][r : r + 1], 16 * r), last)
    edges[...] = jnp.concatenate([sums, last, jnp.zeros((3, COLS), F32)], axis=0)


def window(arrived, ensemble, sent, tile, flat, sums):
    own = lax.axis_index("grp")
    spread = 1.0 / math.sqrt(MEM * GROUPS - 1)
    parts = []
    for i in range(4):
        total = arrived[0, ROWS * i : ROWS * i + ROWS, :].astype(F32)
        for g in range(1, GROUPS):
            total = total + arrived[g, ROWS * i : ROWS * i + ROWS, :].astype(F32)
        parts.append(spread * total)
    for g in range(GROUPS):
        x = arrived[THIRD[g], 4 * ROWS : 5 * ROWS, :].astype(F32)
        for f in range(7):
            sums[f, TILE_ROWS * g : TILE_ROWS * g + TILE_ROWS, :] = x[4 * f : 4 * f + 4]
    lane = lax.broadcasted_iota(jnp.int32, (ROWS, COLS), 1)
    used = jnp.logical_or(lane < RIM, lane >= COLS - RIM)

    def wide(main, packed, place):
        rim = jnp.where(used, turned(packed, -16 * place), 0.0)
        return jnp.concatenate([main, rim], axis=1)

    row = lax.broadcasted_iota(jnp.int32, (ROWS, 2 * COLS), 0)
    rotation = 0.1 + 0.2 * (row.astype(F32) + 0.5) / ROWS
    down = row < ROWS - 1
    up = row > 0
    half_c = 0.5 * COURANT

    def dx(q):
        return half_c * (pltpu.roll(q, 2 * COLS - 1, 1) - pltpu.roll(q, 1, 1))

    def dy(q):
        below = jnp.where(down, pltpu.roll(q, ROWS - 1, 0), 0.0)
        above = jnp.where(up, pltpu.roll(q, 1, 0), 0.0)
        return half_c * (below - above)

    def forward(h, u, w):
        h1 = h - (dx(u) + dy(w))
        return h1, u - dx(h1) + rotation * w, w - dy(h1) - rotation * u

    def backward(bh, bu, bw):
        a = bh + (dx(bu) + dy(bw))
        return a, bu - rotation * bw + dx(a), bw + rotation * bu + dy(a)

    state = tuple(wide(parts[v], parts[3], v) for v in range(3))
    forcing = []
    for t in range(3):
        w_t = wide(sums[t], sums[6], t)
        v_t = wide(sums[3 + t], sums[6], 3 + t)
        forcing.append(w_t * state[0] - v_t)
        if t < 2:
            state = forward(*state)
    zero = jnp.zeros((ROWS, 2 * COLS), F32)
    bh, bu, bw = backward(forcing[2], zero, zero)
    bh, bu, bw = backward(bh + forcing[1], bu, bw)
    bh = bh + forcing[0]
    fin = [x[:, :COLS] for x in (bh, bu, bw)]
    for v in range(3):
        mine = fin[v][:TILE_ROWS]
        for g in range(1, GROUPS):
            mine = jnp.where(own == g, fin[v][TILE_ROWS * g : TILE_ROWS * g + TILE_ROWS], mine)
        tile[v] = mine
    for m in range(MEM):
        total = ensemble[m, 0].astype(F32) * fin[0]
        for v in range(1, 3):
            total = total + ensemble[m, v].astype(F32) * fin[v]
        flat[ROWS * m : ROWS * m + ROWS, :] = total
    by_row(flat, sent, FOURTH)


def assimilate(arrived, ensemble):
    return call(
        window,
        [
            jax.ShapeDtypeStruct((ROWS, SLOTS, COLS), BF16),
            jax.ShapeDtypeStruct((3, TILE_ROWS, COLS), F32),
        ],
        [VMEM((MEM * ROWS, COLS), F32), VMEM((7, ROWS, COLS), F32)],
        2,
    )(arrived, ensemble)


def add_alpha(alpha, arrived, tile, std, control, out, grad, flat):
    spread = 1.0 / math.sqrt(MEM * GROUPS - 1)
    for v in range(3):
        grad[v] = control[v] + std[v] * tile[v]
    for y, place in enumerate(FIFTH):
        flat[SLOTS * y : SLOTS * y + SLOTS, :] = arrived[place].astype(F32)
    for m in range(MEM):
        out[m] = alpha[m] + spread * flat[pl.ds(m, ROWS, stride=SLOTS), :]


def finish(alpha, arrived, tile, std, control):
    return call(
        add_alpha,
        [
            jax.ShapeDtypeStruct((MEM, ROWS, COLS), F32),
            jax.ShapeDtypeStruct((3, TILE_ROWS, COLS), F32),
        ],
        [VMEM((ROWS * SLOTS, COLS), F32)],
        5,
    )(alpha, arrived, tile, std, control)


def swap(x, axis, order):
    return lax.all_to_all(
        x, axis, split_axis=0, concat_axis=0, tiled=True, axis_index_groups=[order]
    )


def per_device(
    alpha, ensemble, static_std, control, loc_spectrum, obs_cell, obs_step, innovation, obs_weight
):
    sent, tiles, edges, weights = first_step(
        alpha, ensemble, loc_spectrum, obs_cell, obs_step, innovation, obs_weight, static_std, control
    )
    rows = swap(sent, SP, FIRST)
    localized = swap(localize(rows, weights, FIRST, SECOND, edges), SP, SECOND)
    summed = swap(partial_sums(ensemble, localized, tiles), "grp", THIRD)
    sent, tile = assimilate(summed, ensemble)
    filtered = swap(localize(swap(sent, SP, FOURTH), weights, FOURTH, FIFTH), SP, FIFTH)
    return finish(alpha, filtered, tile, static_std, control)


def solution(mesh):
    both = P(("grp", SP))
    placed = (
        P("grp", None, SP),
        P("grp", None, None, SP),
        P(None, "grp", SP),
        P(None, "grp", SP),
        P(),
        both,
        both,
        both,
        both,
    )
    return jax.shard_map(
        per_device,
        mesh=mesh,
        in_specs=placed,
        out_specs=(P("grp", None, SP), P(None, "grp", SP)),
        check_vma=False,
    )
```

```python
import functools
import math

import jax
import jax.numpy as jnp
import numpy as np
from jax import lax
from jax.experimental import pallas as pl
from jax.experimental.pallas import tpu as pltpu
from jax.sharding import PartitionSpec as P

SP = "sp"

MEM = 10
SLOTS = 16
ROWS = 32
COLS = 128
BLOCKS = 32
GROUPS = 8
TILE_ROWS = 4
NX = BLOCKS * COLS
KEEP = 1024
ALPHAS = 2 * KEEP // BLOCKS
RIM = 8
SLOT_COUNT = COLS // 16
EXTRA = MEM - SLOT_COUNT
COURANT = 0.4
SUMMED = 3 * ROWS + 16
LOAD = SUMMED + 32

HEADS = (21, 21, 2, 21, 21)


def places(count, head):
    place = list(range(count))
    place[0], place[head] = head, 0
    return place


FIRST, SECOND, THIRD, FOURTH, FIFTH = (
    places(GROUPS // 2 if i == 2 else BLOCKS, head) for i, head in enumerate(HEADS)
)

F32 = jnp.float32
BF16 = jnp.bfloat16
VMEM = pltpu.VMEM


def call(body, out_shape, scratch=(), n_in=1):
    single = not isinstance(out_shape, (list, tuple))
    spec = pl.BlockSpec(memory_space=VMEM)
    return pl.pallas_call(
        body,
        out_shape=out_shape,
        in_specs=[spec] * n_in,
        out_specs=spec if single else [spec] * len(out_shape),
        scratch_shapes=list(scratch),
        compiler_params=pltpu.CompilerParams(vmem_limit_bytes=32 << 20),
    )


def split(table):
    high = table.astype(jnp.bfloat16)
    low = (table - np.asarray(high).astype(np.float64)).astype(jnp.bfloat16)
    return np.asarray(high), np.asarray(low)


def tables():
    j = np.arange(COLS)
    wave = np.concatenate([np.arange(ALPHAS // 2), -1 - np.arange(ALPHAS // 2)])
    angle = 2.0 * np.pi * ((j[:, None] * wave[None, :]) % COLS) / COLS
    c, s = np.cos(angle), np.sin(angle)
    basis = np.concatenate(
        [np.concatenate([c, -s], axis=1), np.concatenate([s, c], axis=1)], axis=0
    )
    turn = 2.0 * np.pi * np.arange(BLOCKS)[:, None] * j[None, :] / NX
    twiddle = np.stack([np.cos(turn), np.sin(turn)]).astype(np.float32)
    high, low = split(basis)
    return high, low, np.ascontiguousarray(high.T), np.ascontiguousarray(low.T), twiddle


def fft(load, start, step, n, sign):
    if n == 1:
        return [load(start)]
    even = fft(load, start, 2 * step, n // 2, sign)
    odd = fft(load, start + step, 2 * step, n // 2, sign)
    low, high = [], []
    for k in range(n // 2):
        er, ei = even[k]
        xr, xi = odd[k]
        if k == 0:
            tr, ti = xr, xi
        elif 4 * k == n:
            tr, ti = (-xi, xr) if sign > 0 else (xi, -xr)
        elif 8 * k == n:
            r = math.sqrt(0.5)
            tr, ti = ((xr - xi) * r, (xr + xi) * r) if sign > 0 else ((xr + xi) * r, (xi - xr) * r)
        elif 8 * k == 3 * n:
            r = math.sqrt(0.5)
            tr, ti = (-(xr + xi) * r, (xr - xi) * r) if sign > 0 else ((xi - xr) * r, -(xr + xi) * r)
        else:
            c = math.cos(2.0 * math.pi * k / n)
            s = sign * math.sin(2.0 * math.pi * k / n)
            tr, ti = xr * c - xi * s, xr * s + xi * c
        low.append((er + tr, ei + ti))
        high.append((er - tr, ei - ti))
    return low + high


def product(x, high, low):
    xh = x.astype(BF16)
    xl = (x - xh.astype(F32)).astype(BF16)
    h = high[...]
    total = jnp.dot(xl, h, preferred_element_type=F32)
    total = total + jnp.dot(xh, low[...], preferred_element_type=F32)
    return total + jnp.dot(xh, h, preferred_element_type=F32)


def slot_of(shape):
    lane = lax.broadcasted_iota(jnp.int32, shape, 1)
    return jnp.right_shift(lane + RIM, 4) & (SLOT_COUNT - 1)


def turned(x, by):
    by = by % COLS
    return x if by == 0 else pltpu.roll(x, by, 1)


def pack_slots(field, count):
    slot = slot_of((count, COLS))
    first = jnp.zeros((count, COLS), F32)
    for m in range(SLOT_COUNT):
        first = jnp.where(slot == m, turned(field(m), 16 * m), first)
    return first


def pack_extra(field, count):
    slot = slot_of((count, COLS))
    extra = jnp.zeros((count, COLS), F32)
    for v in range(3):
        for i in range(EXTRA):
            q = EXTRA * v + i
            extra = jnp.where(slot == q, turned(field(SLOT_COUNT + i, v), 16 * q), extra)
    return extra


def filter_body(rims, come, go, *refs):
    rows, high, low, high_t, low_t, twiddle, weights = refs[:7]
    if rims:
        edges, out, wide, spec, flat, arrived = refs[7:]
    else:
        out, wide, spec = refs[7:]

    def load(p):
        x = rows[come[p]].astype(F32)
        if rims:
            arrived[8 * p : 8 * p + 8, :] = x[8:]
        return x[:8], x[8:]

    for b, (ur, ui) in enumerate(fft(load, 0, 1, BLOCKS, -1)):
        c, s = twiddle[0, b : b + 1, :], twiddle[1, b : b + 1, :]
        wide[8 * b : 8 * b + 8, :COLS] = ur * c + ui * s
        wide[8 * b : 8 * b + 8, COLS:] = ui * c - ur * s
    spec[...] = product(wide[...], high, low)
    for b in range(BLOCKS):
        spec[8 * b : 8 * b + 8, :] = spec[8 * b : 8 * b + 8, :] * weights[b : b + 1, :]
    wide[...] = product(spec[...], high_t, low_t)

    def load_back(b):
        c, s = twiddle[0, b : b + 1, :], twiddle[1, b : b + 1, :]
        yr, yi = wide[8 * b : 8 * b + 8, :COLS], wide[8 * b : 8 * b + 8, COLS:]
        return yr * c - yi * s, yr * s + yi * c

    blocks = fft(load_back, 0, 1, BLOCKS, 1)
    if not rims:
        for p, (yr, yi) in enumerate(blocks):
            out[go[p]] = jnp.concatenate([yr, yi], axis=0).astype(BF16)
        return
    for p, (yr, yi) in enumerate(blocks):
        flat[SLOTS * p : SLOTS * p + 8, :] = yr
        flat[SLOTS * p + 8 : SLOTS * p + 16, :] = yi

    def every(source, place):
        return source[pl.ds(place, BLOCKS, stride=SLOTS), :]

    def edge(i):
        return arrived[pl.ds(MEM - 8 + i, BLOCKS, stride=8), :]

    first = pack_slots(lambda m: every(flat, m), BLOCKS)
    extra = pack_extra(lambda m, v: every(flat, m), BLOCKS)
    extra = extra * edge(3)
    slot = slot_of((BLOCKS, COLS))
    right = (lax.broadcasted_iota(jnp.int32, (BLOCKS, COLS), 1) & 15) < RIM
    side = jnp.zeros((BLOCKS, COLS), F32)
    for v in range(3):
        t = first * edge(v)
        t = t + jnp.where(jnp.right_shift(slot, 1) == v, extra, 0.0)
        for by in (64, 32, 16):
            t = t + turned(t, by)
        side = jnp.where(slot == v, t, side)
    side = jnp.where(right, pltpu.roll(side, BLOCKS - 1, 0), pltpu.roll(side, 1, 0))
    flat[pl.ds(MEM, BLOCKS, stride=SLOTS), :] = side
    own_edges = edges[:5, :]
    for p in range(BLOCKS):
        flat[SLOTS * p + MEM + 1 : SLOTS * p + SLOTS, :] = own_edges
        out[go[p]] = flat[SLOTS * p : SLOTS * p + SLOTS, :].astype(BF16)


def localize(rows, weights, come, go, edges=None):
    rims = edges is not None
    scratch = [VMEM((8 * BLOCKS, 2 * COLS), F32), VMEM((8 * BLOCKS, COLS), F32)]
    if rims:
        scratch += [VMEM((SLOTS * BLOCKS, COLS), F32), VMEM((8 * BLOCKS, COLS), F32)]
    return call(
        functools.partial(filter_body, rims, come, go),
        jax.ShapeDtypeStruct((BLOCKS, SLOTS, COLS), BF16),
        scratch,
        8 if rims else 7,
    )(rows, *tables(), weights, *([edges] if rims else []))


def by_row(flat, out, order):
    for y, place in enumerate(order):
        x = flat[pl.ds(y, MEM, stride=ROWS), :]
        x = jnp.concatenate([x, jnp.zeros((SLOTS - MEM, COLS), F32)], axis=0)
        out[place] = x.astype(BF16)


def pack_weights(loc, out, square, sheet):
    x = loc[...]
    for r in range(4):
        sheet[pl.ds(r, 8, stride=4), :] = turned(x, -BLOCKS * r)
    up = sheet[...]
    lane = lax.broadcasted_iota(jnp.int32, (BLOCKS, COLS), 1)
    row = lax.broadcasted_iota(jnp.int32, (BLOCKS, COLS), 0)
    next_row = jnp.where(row < BLOCKS - 1, pltpu.roll(up, BLOCKS - 1, 0), 0.0)
    down = jnp.where(lane == BLOCKS - 1, turned(next_row, BLOCKS - 1), turned(up, -1))
    both = jnp.concatenate([up, down, jnp.zeros((2 * BLOCKS, COLS), F32)], axis=0)
    square[...] = both.T
    for b in range(BLOCKS):
        sheet[b : b + 1, :] = square[BLOCKS - 1 - b : BLOCKS - b, :]
    h = jnp.where(lane < BLOCKS, square[:BLOCKS, :], jnp.where(lane < 2 * BLOCKS, sheet[...], 0.0))
    h = jnp.where(jnp.logical_and(row == 0, lane == 0), h, 0.5 * h)
    out[...] = h + turned(h, 2 * BLOCKS)


PIECE = 2
SMALL = 7


def first_body(
    alpha, ensemble, loc, cell, step, innovation, weight, std, control,
    out, tiles, edges, weights,
    alpha_v, ens_v, loc_v, cell_v, step_v, innovation_v, weight_v, std_v, control_v,
    flat, square, sheet, small_sem, alpha_sem, ens_sem,
):
    small = [
        pltpu.make_async_copy(a, b, small_sem.at[i])
        for i, (a, b) in enumerate(
            (
                (cell, cell_v),
                (step, step_v),
                (innovation, innovation_v),
                (weight, weight_v),
                (std, std_v),
                (control, control_v),
                (loc, loc_v),
            )
        )
    ]
    count = MEM // PIECE

    def pieces(source, target, sem):
        return [
            pltpu.make_async_copy(
                source.at[pl.ds(PIECE * i, PIECE)], target.at[pl.ds(PIECE * i, PIECE)], sem.at[i]
            )
            for i in range(count)
        ]

    from_alpha = pieces(alpha, alpha_v, alpha_sem)
    from_ensemble = pieces(ensemble, ens_v, ens_sem)
    for copy in small + from_alpha + from_ensemble:
        copy.start()
    for copy in small:
        copy.wait()
    observe(cell_v, step_v, innovation_v, weight_v, std_v, control_v, tiles, edges)
    pack_weights(loc_v, weights, square, sheet)
    for place in range(MEM + 4, SLOTS):
        flat[pl.ds(place, ROWS, stride=SLOTS), :] = jnp.zeros((ROWS, COLS), F32)
    for i, copy in enumerate(from_alpha):
        copy.wait()
        for m in range(PIECE * i, PIECE * i + PIECE):
            flat[pl.ds(m, ROWS, stride=SLOTS), :] = alpha_v[m]
    for copy in from_ensemble:
        copy.wait()
    for v in range(3):
        flat[pl.ds(MEM + v, ROWS, stride=SLOTS), :] = pack_slots(
            lambda m: ens_v[m, v].astype(F32), ROWS
        )
    flat[pl.ds(MEM + 3, ROWS, stride=SLOTS), :] = pack_extra(
        lambda m, v: ens_v[m, v].astype(F32), ROWS
    )
    for y, place in enumerate(FIRST):
        out[place] = flat[SLOTS * y : SLOTS * y + SLOTS, :].astype(BF16)


def first_step(alpha, ensemble, loc, cell, step, innovation, weight, std, control):
    far = pl.BlockSpec(memory_space=pltpu.HBM)
    near = pl.BlockSpec(memory_space=VMEM)
    line = (1, cell.shape[0])
    sems = pltpu.SemaphoreType.DMA
    return pl.pallas_call(
        first_body,
        out_shape=[
            jax.ShapeDtypeStruct((ROWS, SLOTS, COLS), BF16),
            jax.ShapeDtypeStruct((36, COLS), F32),
            jax.ShapeDtypeStruct((8, COLS), F32),
            jax.ShapeDtypeStruct((BLOCKS, COLS), F32),
        ],
        in_specs=[far] * 9,
        out_specs=[near] * 4,
        scratch_shapes=[
            VMEM(alpha.shape, F32),
            VMEM(ensemble.shape, BF16),
            VMEM((8, COLS), F32),
            VMEM(line, jnp.int32),
            VMEM(line, jnp.int32),
            VMEM(line, F32),
            VMEM(line, F32),
            VMEM(std.shape, F32),
            VMEM(control.shape, F32),
            VMEM((ROWS * SLOTS, COLS), F32),
            VMEM((COLS, COLS), F32),
            VMEM((BLOCKS, COLS), F32),
            sems((SMALL,)),
            sems((MEM // PIECE,)),
            sems((MEM // PIECE,)),
        ],
        compiler_params=pltpu.CompilerParams(vmem_limit_bytes=32 << 20),
    )(
        *[
            pltpu.with_memory_space_constraint(a, pltpu.HBM)
            for a in (
                alpha,
                ensemble,
                loc.reshape(8, COLS),
                *[a.reshape(line) for a in (cell, step, innovation, weight)],
                std,
                control,
            )
        ]
    )


def contract(ensemble, arrived, tiles, out, flat):
    own = lax.axis_index("grp")
    column = lax.axis_index(SP)
    unspread = math.sqrt(MEM * GROUPS - 1)
    for y, place in enumerate(SECOND):
        flat[SLOTS * y : SLOTS * y + SLOTS, :] = arrived[place].astype(F32)
    totals = [jnp.zeros((ROWS, COLS), F32)] * 3
    for m in range(MEM):
        field = flat[pl.ds(m, ROWS, stride=SLOTS), :]
        for v in range(3):
            totals[v] = totals[v] + ensemble[m, v].astype(F32) * field
    side = flat[pl.ds(MEM, ROWS, stride=SLOTS), :]
    right = (lax.broadcasted_iota(jnp.int32, (SLOTS, COLS), 1) & 15) < RIM

    def block(y):
        return flat[pl.ds(pl.multiple_of(SLOTS * (y & (BLOCKS - 1)), SLOTS), SLOTS), :]

    after = block(column + 1)
    before = block(column + BLOCKS - 1)
    rim = jnp.where(right, after, before)
    obs_rim = rim[MEM + 1 : MEM + 5]
    last = rim[MEM + 5 : MEM + 6]
    slot = slot_of((TILE_ROWS, COLS))
    static_rim = jnp.where(
        slot == 2,
        jnp.concatenate([turned(last, 16 * (2 - r)) for r in range(TILE_ROWS)], axis=0),
        turned(obs_rim, 32),
    )
    mine = jnp.right_shift(lax.broadcasted_iota(jnp.int32, (ROWS, COLS), 0), 2) == own

    def on_own_rows(tile):
        return jnp.where(mine, unspread * jnp.concatenate([tile] * GROUPS, axis=0), 0.0)

    parts = [
        (totals[v] + on_own_rows(tiles[24 + 4 * v : 28 + 4 * v, :])).astype(BF16)
        for v in range(3)
    ]
    side = side + on_own_rows(static_rim)
    side = jnp.where(slot_of((16, COLS)) < 4, side[:16], turned(side[16:], COLS // 2))
    parts.append(side.astype(BF16))
    parts.append(
        jnp.concatenate([tiles[:24, :], obs_rim, jnp.zeros((4, COLS), F32)], axis=0).astype(BF16)
    )
    payload = jnp.concatenate(parts, axis=0)
    out[...] = payload


def partial_sums(ensemble, arrived, tiles):
    return call(
        contract,
        jax.ShapeDtypeStruct((LOAD, COLS), BF16),
        [VMEM((ROWS * SLOTS, COLS), F32)],
        3,
    )(ensemble, arrived, tiles)


def add_pair(own, other, out):
    low = lax.axis_index("grp") < GROUPS // 2
    x = own[...].astype(F32)
    y = other[...].astype(F32)
    a, b = x[SUMMED:], y[SUMMED:]
    payload = jnp.concatenate(
        [x[:SUMMED] + y[:SUMMED], jnp.where(low, a, b), jnp.where(low, b, a)], axis=0
    ).astype(BF16)
    for g in range(GROUPS // 2):
        out[g] = payload


def pair_sums(own, other):
    return call(
        add_pair, jax.ShapeDtypeStruct((GROUPS // 2, LOAD + 32, COLS), BF16), (), 2
    )(own, other)


def observe(cell, step, innovation, weight, std, control, tiles, edges):
    where_row = jnp.right_shift(cell[...], 12) & (TILE_ROWS - 1)
    key = step[...] * TILE_ROWS + where_row
    column = cell[...] & (COLS - 1)
    w = weight[...]
    wd = w * innovation[...]
    n = 3 * TILE_ROWS
    count = w.shape[1]
    mine = lax.broadcasted_iota(jnp.int32, (n, count), 0) == key
    values = jnp.concatenate([jnp.where(mine, w, 0.0), jnp.where(mine, wd, 0.0)], axis=0)
    high = values.astype(BF16)
    rest = values - high.astype(F32)
    mid = rest.astype(BF16)
    low = (rest - mid.astype(F32)).astype(BF16)
    hot = (lax.broadcasted_iota(jnp.int32, (COLS, count), 0) == column).astype(F32).astype(BF16)
    total = jnp.zeros((2 * n, COLS), F32)
    for piece in (low, mid, high):
        total = total + lax.dot_general(
            piece, hot, (((1,), (1,)), ((), ())), preferred_element_type=F32
        )
    static = [std[v] * control[v] for v in range(3)]
    tiles[:24, :] = total
    for v in range(3):
        tiles[24 + 4 * v : 28 + 4 * v, :] = static[v]
    slot = slot_of((TILE_ROWS, COLS))
    sums = jnp.zeros((TILE_ROWS, COLS), F32)
    for f in range(6):
        sums = jnp.where(slot == f, turned(total[4 * f : 4 * f + 4], 16 * f), sums)
    for v in range(2):
        sums = jnp.where(slot == 6 + v, turned(static[v], 16 * (6 + v)), sums)
    slot = slot_of((1, COLS))
    last = jnp.zeros((1, COLS), F32)
    for r in range(TILE_ROWS):
        last = jnp.where(slot == r, turned(static[2][r : r + 1], 16 * r), last)
    edges[...] = jnp.concatenate([sums, last, jnp.zeros((3, COLS), F32)], axis=0)


def window(arrived, ensemble, sent, tile, flat, sums):
    own = lax.axis_index("grp")
    spread = 1.0 / math.sqrt(MEM * GROUPS - 1)
    total = arrived[0, :SUMMED, :].astype(F32)
    for g in range(1, GROUPS // 2):
        total = total + arrived[g, :SUMMED, :].astype(F32)
    total = spread * total
    parts = [total[ROWS * v : ROWS * v + ROWS] for v in range(3)]
    side = total[3 * ROWS :]
    parts.append(jnp.concatenate([side, turned(side, COLS // 2)], axis=0))
    for g in range(GROUPS):
        x = arrived[THIRD[g % 4], SUMMED + 32 * (g // 4) : LOAD + 32 * (g // 4), :].astype(F32)
        for f in range(7):
            sums[f, TILE_ROWS * g : TILE_ROWS * g + TILE_ROWS, :] = x[4 * f : 4 * f + 4]
    lane = lax.broadcasted_iota(jnp.int32, (ROWS, COLS), 1)
    used = jnp.logical_or(lane < RIM, lane >= COLS - RIM)

    def wide(main, packed, place):
        rim = jnp.where(used, turned(packed, -16 * place), 0.0)
        return jnp.concatenate([main, rim], axis=1)

    row = lax.broadcasted_iota(jnp.int32, (ROWS, 2 * COLS), 0)
    rotation = 0.1 + 0.2 * (row.astype(F32) + 0.5) / ROWS
    down = row < ROWS - 1
    up = row > 0
    half_c = 0.5 * COURANT

    def dx(q):
        return half_c * (pltpu.roll(q, 2 * COLS - 1, 1) - pltpu.roll(q, 1, 1))

    def dy(q):
        below = jnp.where(down, pltpu.roll(q, ROWS - 1, 0), 0.0)
        above = jnp.where(up, pltpu.roll(q, 1, 0), 0.0)
        return half_c * (below - above)

    def forward(h, u, w):
        h1 = h - (dx(u) + dy(w))
        return h1, u - dx(h1) + rotation * w, w - dy(h1) - rotation * u

    def backward(bh, bu, bw):
        a = bh + (dx(bu) + dy(bw))
        return a, bu - rotation * bw + dx(a), bw + rotation * bu + dy(a)

    state = tuple(wide(parts[v], parts[3], v) for v in range(3))
    forcing = []
    for t in range(3):
        w_t = wide(sums[t], sums[6], t)
        v_t = wide(sums[3 + t], sums[6], 3 + t)
        forcing.append(w_t * state[0] - v_t)
        if t < 2:
            state = forward(*state)
    zero = jnp.zeros((ROWS, 2 * COLS), F32)
    bh, bu, bw = backward(forcing[2], zero, zero)
    bh, bu, bw = backward(bh + forcing[1], bu, bw)
    bh = bh + forcing[0]
    fin = [x[:, :COLS] for x in (bh, bu, bw)]
    for v in range(3):
        mine = fin[v][:TILE_ROWS]
        for g in range(1, GROUPS):
            mine = jnp.where(own == g, fin[v][TILE_ROWS * g : TILE_ROWS * g + TILE_ROWS], mine)
        tile[v] = mine
    for m in range(MEM):
        total = ensemble[m, 0].astype(F32) * fin[0]
        for v in range(1, 3):
            total = total + ensemble[m, v].astype(F32) * fin[v]
        flat[ROWS * m : ROWS * m + ROWS, :] = total
    by_row(flat, sent, FOURTH)


def assimilate(arrived, ensemble):
    return call(
        window,
        [
            jax.ShapeDtypeStruct((ROWS, SLOTS, COLS), BF16),
            jax.ShapeDtypeStruct((3, TILE_ROWS, COLS), F32),
        ],
        [VMEM((MEM * ROWS, COLS), F32), VMEM((7, ROWS, COLS), F32)],
        2,
    )(arrived, ensemble)


def add_alpha(alpha, arrived, tile, std, control, out, grad, flat):
    spread = 1.0 / math.sqrt(MEM * GROUPS - 1)
    for v in range(3):
        grad[v] = control[v] + std[v] * tile[v]
    for y, place in enumerate(FIFTH):
        flat[SLOTS * y : SLOTS * y + SLOTS, :] = arrived[place].astype(F32)
    for m in range(MEM):
        out[m] = alpha[m] + spread * flat[pl.ds(m, ROWS, stride=SLOTS), :]


def finish(alpha, arrived, tile, std, control):
    return call(
        add_alpha,
        [
            jax.ShapeDtypeStruct((MEM, ROWS, COLS), F32),
            jax.ShapeDtypeStruct((3, TILE_ROWS, COLS), F32),
        ],
        [VMEM((ROWS * SLOTS, COLS), F32)],
        5,
    )(alpha, arrived, tile, std, control)


def swap(x, axis, order):
    return lax.all_to_all(
        x, axis, split_axis=0, concat_axis=0, tiled=True, axis_index_groups=[order] if axis == SP else [order, [i + GROUPS // 2 for i in order]]
    )


def per_device(
    alpha, ensemble, static_std, control, loc_spectrum, obs_cell, obs_step, innovation, obs_weight
):
    sent, tiles, edges, weights = first_step(
        alpha, ensemble, loc_spectrum, obs_cell, obs_step, innovation, obs_weight, static_std, control
    )
    rows = swap(sent, SP, FIRST)
    localized = swap(localize(rows, weights, FIRST, SECOND, edges), SP, SECOND)
    own = partial_sums(ensemble, localized, tiles)
    other = lax.ppermute(own, "grp", [(i, (i + GROUPS // 2) % GROUPS) for i in range(GROUPS)])
    summed = swap(pair_sums(own, other), "grp", THIRD)
    sent, tile = assimilate(summed, ensemble)
    filtered = swap(localize(swap(sent, SP, FOURTH), weights, FOURTH, FIFTH), SP, FIFTH)
    return finish(alpha, filtered, tile, static_std, control)


def solution(mesh):
    both = P(("grp", SP))
    placed = (
        P("grp", None, SP),
        P("grp", None, None, SP),
        P(None, "grp", SP),
        P(None, "grp", SP),
        P(),
        both,
        both,
        both,
        both,
    )
    return jax.shard_map(
        per_device,
        mesh=mesh,
        in_specs=placed,
        out_specs=(P("grp", None, SP), P(None, "grp", SP)),
        check_vma=False,
    )
```

```python
import functools
import math

import jax
import jax.numpy as jnp
import numpy as np
from jax import lax
from jax.experimental import pallas as pl
from jax.experimental.pallas import tpu as pltpu
from jax.sharding import PartitionSpec as P

SP = "sp"

MEM = 10
SLOTS = 16
ROWS = 32
COLS = 128
BLOCKS = 32
GROUPS = 8
TILE_ROWS = 4
NX = BLOCKS * COLS
KEEP = 1024
ALPHAS = 2 * KEEP // BLOCKS
RIM = 8
SLOT_COUNT = COLS // 16
EXTRA = MEM - SLOT_COUNT
COURANT = 0.4
SUMMED = 3 * ROWS + 16
LOAD = SUMMED + 32

HEADS = (21, 21, 2, 21, 21)


def places(count, head):
    place = list(range(count))
    place[0], place[head] = head, 0
    return place


FIRST, SECOND, THIRD, FOURTH, FIFTH = (
    places(GROUPS // 2 if i == 2 else BLOCKS, head) for i, head in enumerate(HEADS)
)

F32 = jnp.float32
BF16 = jnp.bfloat16
VMEM = pltpu.VMEM


def call(body, out_shape, scratch=(), n_in=1):
    single = not isinstance(out_shape, (list, tuple))
    spec = pl.BlockSpec(memory_space=VMEM)
    return pl.pallas_call(
        body,
        out_shape=out_shape,
        in_specs=[spec] * n_in,
        out_specs=spec if single else [spec] * len(out_shape),
        scratch_shapes=list(scratch),
        compiler_params=pltpu.CompilerParams(vmem_limit_bytes=32 << 20),
    )


def split(table):
    high = table.astype(jnp.bfloat16)
    low = (table - np.asarray(high).astype(np.float64)).astype(jnp.bfloat16)
    return np.asarray(high), np.asarray(low)


def tables():
    j = np.arange(COLS)
    wave = np.concatenate([np.arange(ALPHAS // 2), -1 - np.arange(ALPHAS // 2)])
    angle = 2.0 * np.pi * ((j[:, None] * wave[None, :]) % COLS) / COLS
    c, s = np.cos(angle), np.sin(angle)
    basis = np.concatenate(
        [np.concatenate([c, -s], axis=1), np.concatenate([s, c], axis=1)], axis=0
    )
    turn = 2.0 * np.pi * np.arange(BLOCKS)[:, None] * j[None, :] / NX
    twiddle = np.stack([np.cos(turn), np.sin(turn)]).astype(np.float32)
    high, low = split(basis)
    return high, low, np.ascontiguousarray(high.T), np.ascontiguousarray(low.T), twiddle


def fft(load, start, step, n, sign):
    if n == 1:
        return [load(start)]
    even = fft(load, start, 2 * step, n // 2, sign)
    odd = fft(load, start + step, 2 * step, n // 2, sign)
    low, high = [], []
    for k in range(n // 2):
        er, ei = even[k]
        xr, xi = odd[k]
        if k == 0:
            tr, ti = xr, xi
        elif 4 * k == n:
            tr, ti = (-xi, xr) if sign > 0 else (xi, -xr)
        elif 8 * k == n:
            r = math.sqrt(0.5)
            tr, ti = ((xr - xi) * r, (xr + xi) * r) if sign > 0 else ((xr + xi) * r, (xi - xr) * r)
        elif 8 * k == 3 * n:
            r = math.sqrt(0.5)
            tr, ti = (-(xr + xi) * r, (xr - xi) * r) if sign > 0 else ((xi - xr) * r, -(xr + xi) * r)
        else:
            c = math.cos(2.0 * math.pi * k / n)
            s = sign * math.sin(2.0 * math.pi * k / n)
            tr, ti = xr * c - xi * s, xr * s + xi * c
        low.append((er + tr, ei + ti))
        high.append((er - tr, ei - ti))
    return low + high


def product(x, high, low):
    xh = x.astype(BF16)
    xl = (x - xh.astype(F32)).astype(BF16)
    h = high[...]
    n = x.shape[0]
    both = jnp.dot(jnp.concatenate([xl, xh], axis=0), h, preferred_element_type=F32)
    return both[:n] + jnp.dot(xh, low[...], preferred_element_type=F32) + both[n:]


def slot_of(shape):
    lane = lax.broadcasted_iota(jnp.int32, shape, 1)
    return jnp.right_shift(lane + RIM, 4) & (SLOT_COUNT - 1)


def turned(x, by):
    by = by % COLS
    return x if by == 0 else pltpu.roll(x, by, 1)


def pack_slots(field, count):
    slot = slot_of((count, COLS))
    first = jnp.zeros((count, COLS), F32)
    for m in range(SLOT_COUNT):
        first = jnp.where(slot == m, turned(field(m), 16 * m), first)
    return first


def pack_extra(field, count):
    slot = slot_of((count, COLS))
    extra = jnp.zeros((count, COLS), F32)
    for v in range(3):
        for i in range(EXTRA):
            q = EXTRA * v + i
            extra = jnp.where(slot == q, turned(field(SLOT_COUNT + i, v), 16 * q), extra)
    return extra


def filter_body(rims, come, go, *refs):
    rows, high, low, high_t, low_t, twiddle, weights = refs[:7]
    if rims:
        edges, out, wide, spec, flat, arrived = refs[7:]
    else:
        out, wide, spec = refs[7:]

    def load(p):
        x = rows[come[p]].astype(F32)
        if rims:
            arrived[8 * p : 8 * p + 8, :] = x[8:]
        return x[:8], x[8:]

    for b, (ur, ui) in enumerate(fft(load, 0, 1, BLOCKS, -1)):
        c, s = twiddle[0, b : b + 1, :], twiddle[1, b : b + 1, :]
        wide[8 * b : 8 * b + 8, :COLS] = ur * c + ui * s
        wide[8 * b : 8 * b + 8, COLS:] = ui * c - ur * s
    spec[...] = product(wide[...], high, low)
    for b in range(BLOCKS):
        spec[8 * b : 8 * b + 8, :] = spec[8 * b : 8 * b + 8, :] * weights[b : b + 1, :]
    wide[...] = product(spec[...], high_t, low_t)

    def load_back(b):
        c, s = twiddle[0, b : b + 1, :], twiddle[1, b : b + 1, :]
        yr, yi = wide[8 * b : 8 * b + 8, :COLS], wide[8 * b : 8 * b + 8, COLS:]
        return yr * c - yi * s, yr * s + yi * c

    blocks = fft(load_back, 0, 1, BLOCKS, 1)
    if not rims:
        for p, (yr, yi) in enumerate(blocks):
            out[go[p]] = jnp.concatenate([yr, yi], axis=0).astype(BF16)
        return
    for p, (yr, yi) in enumerate(blocks):
        flat[SLOTS * p : SLOTS * p + 8, :] = yr
        flat[SLOTS * p + 8 : SLOTS * p + 16, :] = yi

    def every(source, place):
        return source[pl.ds(place, BLOCKS, stride=SLOTS), :]

    def edge(i):
        return arrived[pl.ds(MEM - 8 + i, BLOCKS, stride=8), :]

    first = pack_slots(lambda m: every(flat, m), BLOCKS)
    extra = pack_extra(lambda m, v: every(flat, m), BLOCKS)
    extra = extra * edge(3)
    slot = slot_of((BLOCKS, COLS))
    right = (lax.broadcasted_iota(jnp.int32, (BLOCKS, COLS), 1) & 15) < RIM
    side = jnp.zeros((BLOCKS, COLS), F32)
    for v in range(3):
        t = first * edge(v)
        t = t + jnp.where(jnp.right_shift(slot, 1) == v, extra, 0.0)
        for by in (64, 32, 16):
            t = t + turned(t, by)
        side = jnp.where(slot == v, t, side)
    side = jnp.where(right, pltpu.roll(side, BLOCKS - 1, 0), pltpu.roll(side, 1, 0))
    flat[pl.ds(MEM, BLOCKS, stride=SLOTS), :] = side
    own_edges = edges[:5, :]
    for p in range(BLOCKS):
        flat[SLOTS * p + MEM + 1 : SLOTS * p + SLOTS, :] = own_edges
        out[go[p]] = flat[SLOTS * p : SLOTS * p + SLOTS, :].astype(BF16)


def localize(rows, weights, come, go, edges=None):
    rims = edges is not None
    scratch = [VMEM((8 * BLOCKS, 2 * COLS), F32), VMEM((8 * BLOCKS, COLS), F32)]
    if rims:
        scratch += [VMEM((SLOTS * BLOCKS, COLS), F32), VMEM((8 * BLOCKS, COLS), F32)]
    return call(
        functools.partial(filter_body, rims, come, go),
        jax.ShapeDtypeStruct((BLOCKS, SLOTS, COLS), BF16),
        scratch,
        8 if rims else 7,
    )(rows, *tables(), weights, *([edges] if rims else []))


def by_row(flat, out, order):
    for y, place in enumerate(order):
        x = flat[pl.ds(y, MEM, stride=ROWS), :]
        x = jnp.concatenate([x, jnp.zeros((SLOTS - MEM, COLS), F32)], axis=0)
        out[place] = x.astype(BF16)


def pack_weights(loc, out, square, sheet):
    x = loc[...]
    for r in range(4):
        sheet[pl.ds(r, 8, stride=4), :] = turned(x, -BLOCKS * r)
    up = sheet[...]
    lane = lax.broadcasted_iota(jnp.int32, (BLOCKS, COLS), 1)
    row = lax.broadcasted_iota(jnp.int32, (BLOCKS, COLS), 0)
    next_row = jnp.where(row < BLOCKS - 1, pltpu.roll(up, BLOCKS - 1, 0), 0.0)
    down = jnp.where(lane == BLOCKS - 1, turned(next_row, BLOCKS - 1), turned(up, -1))
    both = jnp.concatenate([up, down, jnp.zeros((2 * BLOCKS, COLS), F32)], axis=0)
    square[...] = both.T
    for b in range(BLOCKS):
        sheet[b : b + 1, :] = square[BLOCKS - 1 - b : BLOCKS - b, :]
    h = jnp.where(lane < BLOCKS, square[:BLOCKS, :], jnp.where(lane < 2 * BLOCKS, sheet[...], 0.0))
    h = jnp.where(jnp.logical_and(row == 0, lane == 0), h, 0.5 * h)
    out[...] = h + turned(h, 2 * BLOCKS)


PIECE = 10
SMALL = 7


def first_body(
    alpha, ensemble, loc, cell, step, innovation, weight, std, control,
    out, tiles, edges, weights,
    alpha_v, ens_v, loc_v, cell_v, step_v, innovation_v, weight_v, std_v, control_v,
    flat, square, sheet, small_sem, alpha_sem, ens_sem,
):
    small = [
        pltpu.make_async_copy(a, b, small_sem.at[i])
        for i, (a, b) in enumerate(
            (
                (cell, cell_v),
                (step, step_v),
                (innovation, innovation_v),
                (weight, weight_v),
                (std, std_v),
                (control, control_v),
                (loc, loc_v),
            )
        )
    ]
    count = MEM // PIECE

    def pieces(source, target, sem):
        return [
            pltpu.make_async_copy(
                source.at[pl.ds(PIECE * i, PIECE)], target.at[pl.ds(PIECE * i, PIECE)], sem.at[i]
            )
            for i in range(count)
        ]

    from_alpha = pieces(alpha, alpha_v, alpha_sem)
    from_ensemble = pieces(ensemble, ens_v, ens_sem)
    for copy in small + from_alpha + from_ensemble:
        copy.start()
    for copy in small:
        copy.wait()
    observe(cell_v, step_v, innovation_v, weight_v, std_v, control_v, tiles, edges)
    pack_weights(loc_v, weights, square, sheet)
    for place in range(MEM + 4, SLOTS):
        flat[pl.ds(place, ROWS, stride=SLOTS), :] = jnp.zeros((ROWS, COLS), F32)
    for i, copy in enumerate(from_alpha):
        copy.wait()
        for m in range(PIECE * i, PIECE * i + PIECE):
            flat[pl.ds(m, ROWS, stride=SLOTS), :] = alpha_v[m]
    for copy in from_ensemble:
        copy.wait()
    for v in range(3):
        flat[pl.ds(MEM + v, ROWS, stride=SLOTS), :] = pack_slots(
            lambda m: ens_v[m, v].astype(F32), ROWS
        )
    flat[pl.ds(MEM + 3, ROWS, stride=SLOTS), :] = pack_extra(
        lambda m, v: ens_v[m, v].astype(F32), ROWS
    )
    for y, place in enumerate(FIRST):
        out[place] = flat[SLOTS * y : SLOTS * y + SLOTS, :].astype(BF16)


def first_step(alpha, ensemble, loc, cell, step, innovation, weight, std, control):
    far = pl.BlockSpec(memory_space=pltpu.HBM)
    near = pl.BlockSpec(memory_space=VMEM)
    line = (1, cell.shape[0])
    sems = pltpu.SemaphoreType.DMA
    return pl.pallas_call(
        first_body,
        out_shape=[
            jax.ShapeDtypeStruct((ROWS, SLOTS, COLS), BF16),
            jax.ShapeDtypeStruct((36, COLS), F32),
            jax.ShapeDtypeStruct((8, COLS), F32),
            jax.ShapeDtypeStruct((BLOCKS, COLS), F32),
        ],
        in_specs=[far] * 9,
        out_specs=[near] * 4,
        scratch_shapes=[
            VMEM(alpha.shape, F32),
            VMEM(ensemble.shape, BF16),
            VMEM((8, COLS), F32),
            VMEM(line, jnp.int32),
            VMEM(line, jnp.int32),
            VMEM(line, F32),
            VMEM(line, F32),
            VMEM(std.shape, F32),
            VMEM(control.shape, F32),
            VMEM((ROWS * SLOTS, COLS), F32),
            VMEM((COLS, COLS), F32),
            VMEM((BLOCKS, COLS), F32),
            sems((SMALL,)),
            sems((MEM // PIECE,)),
            sems((MEM // PIECE,)),
        ],
        compiler_params=pltpu.CompilerParams(vmem_limit_bytes=32 << 20),
    )(
        *[
            pltpu.with_memory_space_constraint(a, pltpu.HBM)
            for a in (
                alpha,
                ensemble,
                loc.reshape(8, COLS),
                *[a.reshape(line) for a in (cell, step, innovation, weight)],
                std,
                control,
            )
        ]
    )


def contract(ensemble, arrived, tiles, out, flat):
    own = lax.axis_index("grp")
    column = lax.axis_index(SP)
    unspread = math.sqrt(MEM * GROUPS - 1)
    for y, place in enumerate(SECOND):
        flat[SLOTS * y : SLOTS * y + SLOTS, :] = arrived[place].astype(F32)
    totals = [jnp.zeros((ROWS, COLS), F32)] * 3
    for m in range(MEM):
        field = flat[pl.ds(m, ROWS, stride=SLOTS), :]
        for v in range(3):
            totals[v] = totals[v] + ensemble[m, v].astype(F32) * field
    side = flat[pl.ds(MEM, ROWS, stride=SLOTS), :]
    right = (lax.broadcasted_iota(jnp.int32, (SLOTS, COLS), 1) & 15) < RIM

    def block(y):
        return flat[pl.ds(pl.multiple_of(SLOTS * (y & (BLOCKS - 1)), SLOTS), SLOTS), :]

    after = block(column + 1)
    before = block(column + BLOCKS - 1)
    rim = jnp.where(right, after, before)
    obs_rim = rim[MEM + 1 : MEM + 5]
    last = rim[MEM + 5 : MEM + 6]
    slot = slot_of((TILE_ROWS, COLS))
    static_rim = jnp.where(
        slot == 2,
        jnp.concatenate([turned(last, 16 * (2 - r)) for r in range(TILE_ROWS)], axis=0),
        turned(obs_rim, 32),
    )
    mine = jnp.right_shift(lax.broadcasted_iota(jnp.int32, (ROWS, COLS), 0), 2) == own

    def on_own_rows(tile):
        return jnp.where(mine, unspread * jnp.concatenate([tile] * GROUPS, axis=0), 0.0)

    parts = [
        (totals[v] + on_own_rows(tiles[24 + 4 * v : 28 + 4 * v, :])).astype(BF16)
        for v in range(3)
    ]
    side = side + on_own_rows(static_rim)
    side = jnp.where(slot_of((16, COLS)) < 4, side[:16], turned(side[16:], COLS // 2))
    parts.append(side.astype(BF16))
    parts.append(
        jnp.concatenate([tiles[:24, :], obs_rim, jnp.zeros((4, COLS), F32)], axis=0).astype(BF16)
    )
    payload = jnp.concatenate(parts, axis=0)
    out[...] = payload


def partial_sums(ensemble, arrived, tiles):
    return call(
        contract,
        jax.ShapeDtypeStruct((LOAD, COLS), BF16),
        [VMEM((ROWS * SLOTS, COLS), F32)],
        3,
    )(ensemble, arrived, tiles)


def add_pair(own, other, out):
    low = lax.axis_index("grp") < GROUPS // 2
    x = own[...].astype(F32)
    y = other[...].astype(F32)
    a, b = x[SUMMED:], y[SUMMED:]
    payload = jnp.concatenate(
        [x[:SUMMED] + y[:SUMMED], jnp.where(low, a, b), jnp.where(low, b, a)], axis=0
    ).astype(BF16)
    for g in range(GROUPS // 2):
        out[g] = payload


def pair_sums(own, other):
    return call(
        add_pair, jax.ShapeDtypeStruct((GROUPS // 2, LOAD + 32, COLS), BF16), (), 2
    )(own, other)


def observe(cell, step, innovation, weight, std, control, tiles, edges):
    where_row = jnp.right_shift(cell[...], 12) & (TILE_ROWS - 1)
    key = step[...] * TILE_ROWS + where_row
    column = cell[...] & (COLS - 1)
    w = weight[...]
    wd = w * innovation[...]
    n = 3 * TILE_ROWS
    count = w.shape[1]
    mine = lax.broadcasted_iota(jnp.int32, (n, count), 0) == key
    values = jnp.concatenate([jnp.where(mine, w, 0.0), jnp.where(mine, wd, 0.0)], axis=0)
    high = values.astype(BF16)
    rest = values - high.astype(F32)
    mid = rest.astype(BF16)
    low = (rest - mid.astype(F32)).astype(BF16)
    hot = (lax.broadcasted_iota(jnp.int32, (COLS, count), 0) == column).astype(F32).astype(BF16)
    pieces = lax.dot_general(
        jnp.concatenate([low.astype(F32), mid.astype(F32), high.astype(F32)], axis=0).astype(BF16),
        hot,
        (((1,), (1,)), ((), ())),
        preferred_element_type=F32,
    )
    total = pieces[: 2 * n] + pieces[2 * n : 4 * n] + pieces[4 * n :]
    static = [std[v] * control[v] for v in range(3)]
    tiles[:24, :] = total
    for v in range(3):
        tiles[24 + 4 * v : 28 + 4 * v, :] = static[v]
    slot = slot_of((TILE_ROWS, COLS))
    sums = jnp.zeros((TILE_ROWS, COLS), F32)
    for f in range(6):
        sums = jnp.where(slot == f, turned(total[4 * f : 4 * f + 4], 16 * f), sums)
    for v in range(2):
        sums = jnp.where(slot == 6 + v, turned(static[v], 16 * (6 + v)), sums)
    slot = slot_of((1, COLS))
    last = jnp.zeros((1, COLS), F32)
    for r in range(TILE_ROWS):
        last = jnp.where(slot == r, turned(static[2][r : r + 1], 16 * r), last)
    edges[...] = jnp.concatenate([sums, last, jnp.zeros((3, COLS), F32)], axis=0)


def window(arrived, ensemble, sent, tile, flat, sums):
    own = lax.axis_index("grp")
    spread = 1.0 / math.sqrt(MEM * GROUPS - 1)
    total = arrived[0, :SUMMED, :].astype(F32)
    for g in range(1, GROUPS // 2):
        total = total + arrived[g, :SUMMED, :].astype(F32)
    total = spread * total
    parts = [total[ROWS * v : ROWS * v + ROWS] for v in range(3)]
    side = total[3 * ROWS :]
    parts.append(jnp.concatenate([side, turned(side, COLS // 2)], axis=0))
    for g in range(GROUPS):
        x = arrived[THIRD[g % 4], SUMMED + 32 * (g // 4) : LOAD + 32 * (g // 4), :].astype(F32)
        for f in range(7):
            sums[f, TILE_ROWS * g : TILE_ROWS * g + TILE_ROWS, :] = x[4 * f : 4 * f + 4]
    lane = lax.broadcasted_iota(jnp.int32, (ROWS, COLS), 1)
    used = jnp.logical_or(lane < RIM, lane >= COLS - RIM)

    def wide(main, packed, place):
        rim = jnp.where(used, turned(packed, -16 * place), 0.0)
        return jnp.concatenate([main, rim], axis=1)

    row = lax.broadcasted_iota(jnp.int32, (ROWS, 2 * COLS), 0)
    rotation = 0.1 + 0.2 * (row.astype(F32) + 0.5) / ROWS
    down = row < ROWS - 1
    up = row > 0
    half_c = 0.5 * COURANT

    def dx(q):
        return half_c * (pltpu.roll(q, 2 * COLS - 1, 1) - pltpu.roll(q, 1, 1))

    def dy(q):
        below = jnp.where(down, pltpu.roll(q, ROWS - 1, 0), 0.0)
        above = jnp.where(up, pltpu.roll(q, 1, 0), 0.0)
        return half_c * (below - above)

    def forward(h, u, w):
        h1 = h - (dx(u) + dy(w))
        return h1, u - dx(h1) + rotation * w, w - dy(h1) - rotation * u

    def backward(bh, bu, bw):
        a = bh + (dx(bu) + dy(bw))
        return a, bu - rotation * bw + dx(a), bw + rotation * bu + dy(a)

    state = tuple(wide(parts[v], parts[3], v) for v in range(3))
    forcing = []
    for t in range(3):
        w_t = wide(sums[t], sums[6], t)
        v_t = wide(sums[3 + t], sums[6], 3 + t)
        forcing.append(w_t * state[0] - v_t)
        if t < 2:
            state = forward(*state)
    zero = jnp.zeros((ROWS, 2 * COLS), F32)
    bh, bu, bw = backward(forcing[2], zero, zero)
    bh, bu, bw = backward(bh + forcing[1], bu, bw)
    bh = bh + forcing[0]
    fin = [x[:, :COLS] for x in (bh, bu, bw)]
    for v in range(3):
        mine = fin[v][:TILE_ROWS]
        for g in range(1, GROUPS):
            mine = jnp.where(own == g, fin[v][TILE_ROWS * g : TILE_ROWS * g + TILE_ROWS], mine)
        tile[v] = mine
    for m in range(MEM):
        total = ensemble[m, 0].astype(F32) * fin[0]
        for v in range(1, 3):
            total = total + ensemble[m, v].astype(F32) * fin[v]
        flat[ROWS * m : ROWS * m + ROWS, :] = total
    by_row(flat, sent, FOURTH)


def assimilate(arrived, ensemble):
    return call(
        window,
        [
            jax.ShapeDtypeStruct((ROWS, SLOTS, COLS), BF16),
            jax.ShapeDtypeStruct((3, TILE_ROWS, COLS), F32),
        ],
        [VMEM((MEM * ROWS, COLS), F32), VMEM((7, ROWS, COLS), F32)],
        2,
    )(arrived, ensemble)


def add_alpha(alpha, arrived, tile, std, control, out, grad, flat):
    spread = 1.0 / math.sqrt(MEM * GROUPS - 1)
    for v in range(3):
        grad[v] = control[v] + std[v] * tile[v]
    for y, place in enumerate(FIFTH):
        flat[SLOTS * y : SLOTS * y + SLOTS, :] = arrived[place].astype(F32)
    for m in range(MEM):
        out[m] = alpha[m] + spread * flat[pl.ds(m, ROWS, stride=SLOTS), :]


def finish(alpha, arrived, tile, std, control):
    return call(
        add_alpha,
        [
            jax.ShapeDtypeStruct((MEM, ROWS, COLS), F32),
            jax.ShapeDtypeStruct((3, TILE_ROWS, COLS), F32),
        ],
        [VMEM((ROWS * SLOTS, COLS), F32)],
        5,
    )(alpha, arrived, tile, std, control)


def swap(x, axis, order):
    return lax.all_to_all(
        x, axis, split_axis=0, concat_axis=0, tiled=True, axis_index_groups=[order] if axis == SP else [order, [i + GROUPS // 2 for i in order]]
    )


def per_device(
    alpha, ensemble, static_std, control, loc_spectrum, obs_cell, obs_step, innovation, obs_weight
):
    sent, tiles, edges, weights = first_step(
        alpha, ensemble, loc_spectrum, obs_cell, obs_step, innovation, obs_weight, static_std, control
    )
    rows = swap(sent, SP, FIRST)
    localized = swap(localize(rows, weights, FIRST, SECOND, edges), SP, SECOND)
    own = partial_sums(ensemble, localized, tiles)
    other = lax.ppermute(own, "grp", [(i, (i + GROUPS // 2) % GROUPS) for i in range(GROUPS)])
    summed = swap(pair_sums(own, other), "grp", THIRD)
    sent, tile = assimilate(summed, ensemble)
    filtered = swap(localize(swap(sent, SP, FOURTH), weights, FOURTH, FIFTH), SP, FIFTH)
    return finish(alpha, filtered, tile, static_std, control)


def solution(mesh):
    both = P(("grp", SP))
    placed = (
        P("grp", None, SP),
        P("grp", None, None, SP),
        P(None, "grp", SP),
        P(None, "grp", SP),
        P(),
        both,
        both,
        both,
        both,
    )
    return jax.shard_map(
        per_device,
        mesh=mesh,
        in_specs=placed,
        out_specs=(P("grp", None, SP), P(None, "grp", SP)),
        check_vma=False,
    )
```

```python
import functools
import math

import jax
import jax.numpy as jnp
import numpy as np
from jax import lax
from jax.experimental import pallas as pl
from jax.experimental.pallas import tpu as pltpu
from jax.sharding import PartitionSpec as P

SP = "sp"

MEM = 10
SLOTS = 16
ROWS = 32
COLS = 128
BLOCKS = 32
GROUPS = 8
TILE_ROWS = 4
NX = BLOCKS * COLS
KEEP = 1024
ALPHAS = 2 * KEEP // BLOCKS
RIM = 8
SLOT_COUNT = COLS // 16
EXTRA = MEM - SLOT_COUNT
COURANT = 0.4
SUMMED = 3 * ROWS + 16
LOAD = SUMMED + 32

HEADS = (21, 21, 2, 21, 21)


def places(count, head):
    place = list(range(count))
    place[0], place[head] = head, 0
    return place


FIRST, SECOND, THIRD, FOURTH, FIFTH = (
    places(GROUPS // 2 if i == 2 else BLOCKS, head) for i, head in enumerate(HEADS)
)

F32 = jnp.float32
BF16 = jnp.bfloat16
VMEM = pltpu.VMEM


def call(body, out_shape, scratch=(), n_in=1):
    single = not isinstance(out_shape, (list, tuple))
    spec = pl.BlockSpec(memory_space=VMEM)
    return pl.pallas_call(
        body,
        out_shape=out_shape,
        in_specs=[spec] * n_in,
        out_specs=spec if single else [spec] * len(out_shape),
        scratch_shapes=list(scratch),
        compiler_params=pltpu.CompilerParams(vmem_limit_bytes=32 << 20),
    )


def split(table):
    high = table.astype(jnp.bfloat16)
    low = (table - np.asarray(high).astype(np.float64)).astype(jnp.bfloat16)
    return np.asarray(high), np.asarray(low)


def tables():
    j = np.arange(COLS)
    wave = np.concatenate([np.arange(ALPHAS // 2), -1 - np.arange(ALPHAS // 2)])
    angle = 2.0 * np.pi * ((j[:, None] * wave[None, :]) % COLS) / COLS
    c, s = np.cos(angle), np.sin(angle)
    basis = np.concatenate(
        [np.concatenate([c, -s], axis=1), np.concatenate([s, c], axis=1)], axis=0
    )
    turn = 2.0 * np.pi * np.arange(BLOCKS)[:, None] * j[None, :] / NX
    twiddle = np.stack([np.cos(turn), np.sin(turn)]).astype(np.float32)
    high, low = split(basis)
    return high, low, np.ascontiguousarray(high.T), np.ascontiguousarray(low.T), twiddle


def fft(load, start, step, n, sign):
    if n == 1:
        return [load(start)]
    even = fft(load, start, 2 * step, n // 2, sign)
    odd = fft(load, start + step, 2 * step, n // 2, sign)
    low, high = [], []
    for k in range(n // 2):
        er, ei = even[k]
        xr, xi = odd[k]
        if k == 0:
            tr, ti = xr, xi
        elif 4 * k == n:
            tr, ti = (-xi, xr) if sign > 0 else (xi, -xr)
        elif 8 * k == n:
            r = math.sqrt(0.5)
            tr, ti = ((xr - xi) * r, (xr + xi) * r) if sign > 0 else ((xr + xi) * r, (xi - xr) * r)
        elif 8 * k == 3 * n:
            r = math.sqrt(0.5)
            tr, ti = (-(xr + xi) * r, (xr - xi) * r) if sign > 0 else ((xi - xr) * r, -(xr + xi) * r)
        else:
            c = math.cos(2.0 * math.pi * k / n)
            s = sign * math.sin(2.0 * math.pi * k / n)
            tr, ti = xr * c - xi * s, xr * s + xi * c
        low.append((er + tr, ei + ti))
        high.append((er - tr, ei - ti))
    return low + high


def product(x, high, low):
    xh = x.astype(BF16)
    xl = (x - xh.astype(F32)).astype(BF16)
    h = high[...]
    n = x.shape[0]
    both = jnp.dot(jnp.concatenate([xl, xh], axis=0), h, preferred_element_type=F32)
    return both[:n] + jnp.dot(xh, low[...], preferred_element_type=F32) + both[n:]


def slot_of(shape):
    lane = lax.broadcasted_iota(jnp.int32, shape, 1)
    return jnp.right_shift(lane + RIM, 4) & (SLOT_COUNT - 1)


def turned(x, by):
    by = by % COLS
    return x if by == 0 else pltpu.roll(x, by, 1)


def pack_slots(field, count):
    slot = slot_of((count, COLS))
    first = jnp.zeros((count, COLS), F32)
    for m in range(SLOT_COUNT):
        first = jnp.where(slot == m, turned(field(m), 16 * m), first)
    return first


def pack_extra(field, count):
    slot = slot_of((count, COLS))
    extra = jnp.zeros((count, COLS), F32)
    for v in range(3):
        for i in range(EXTRA):
            q = EXTRA * v + i
            extra = jnp.where(slot == q, turned(field(SLOT_COUNT + i, v), 16 * q), extra)
    return extra


def filter_body(rims, come, go, *refs):
    rows, high, low, high_t, low_t, twiddle, weights = refs[:7]
    if rims:
        edges, out, wide, spec, flat, arrived = refs[7:]
    else:
        out, wide, spec = refs[7:]

    def load(p):
        x = rows[come[p]].astype(F32)
        if rims:
            arrived[8 * p : 8 * p + 8, :] = x[8:]
        return x[:8], x[8:]

    for b, (ur, ui) in enumerate(fft(load, 0, 1, BLOCKS, -1)):
        c, s = twiddle[0, b : b + 1, :], twiddle[1, b : b + 1, :]
        wide[8 * b : 8 * b + 8, :COLS] = ur * c + ui * s
        wide[8 * b : 8 * b + 8, COLS:] = ui * c - ur * s
    spec[...] = product(wide[...], high, low)
    for b in range(BLOCKS):
        spec[8 * b : 8 * b + 8, :] = spec[8 * b : 8 * b + 8, :] * weights[b : b + 1, :]
    wide[...] = product(spec[...], high_t, low_t)

    def load_back(b):
        c, s = twiddle[0, b : b + 1, :], twiddle[1, b : b + 1, :]
        yr, yi = wide[8 * b : 8 * b + 8, :COLS], wide[8 * b : 8 * b + 8, COLS:]
        return yr * c - yi * s, yr * s + yi * c

    blocks = fft(load_back, 0, 1, BLOCKS, 1)
    if not rims:
        for p, (yr, yi) in enumerate(blocks):
            out[go[p]] = jnp.concatenate([yr, yi], axis=0).astype(BF16)
        return
    for p, (yr, yi) in enumerate(blocks):
        flat[SLOTS * p : SLOTS * p + 8, :] = yr
        flat[SLOTS * p + 8 : SLOTS * p + 16, :] = yi

    def every(source, place):
        return source[pl.ds(place, BLOCKS, stride=SLOTS), :]

    def edge(i):
        return arrived[pl.ds(MEM - 8 + i, BLOCKS, stride=8), :]

    first = pack_slots(lambda m: every(flat, m), BLOCKS)
    extra = pack_extra(lambda m, v: every(flat, m), BLOCKS)
    extra = extra * edge(3)
    slot = slot_of((BLOCKS, COLS))
    right = (lax.broadcasted_iota(jnp.int32, (BLOCKS, COLS), 1) & 15) < RIM
    side = jnp.zeros((BLOCKS, COLS), F32)
    for v in range(3):
        t = first * edge(v)
        t = t + jnp.where(jnp.right_shift(slot, 1) == v, extra, 0.0)
        for by in (64, 32, 16):
            t = t + turned(t, by)
        side = jnp.where(slot == v, t, side)
    side = jnp.where(right, pltpu.roll(side, BLOCKS - 1, 0), pltpu.roll(side, 1, 0))
    spec[:BLOCKS, :] = side
    sub = lax.broadcasted_iota(jnp.int32, (8, COLS), 0)
    own_edges = pltpu.roll(edges[...], MEM - 8 + 1, 0)
    for p in range(BLOCKS):
        late = flat[SLOTS * p + 8 : SLOTS * p + SLOTS, :]
        late = jnp.where(sub < MEM - 8, late, own_edges)
        late = jnp.where(sub == MEM - 8, spec[p : p + 1, :], late)
        out[go[p]] = jnp.concatenate([flat[SLOTS * p : SLOTS * p + 8, :], late], axis=0).astype(BF16)


def localize(rows, weights, come, go, edges=None):
    rims = edges is not None
    scratch = [VMEM((8 * BLOCKS, 2 * COLS), F32), VMEM((8 * BLOCKS, COLS), F32)]
    if rims:
        scratch += [VMEM((SLOTS * BLOCKS, COLS), F32), VMEM((8 * BLOCKS, COLS), F32)]
    return call(
        functools.partial(filter_body, rims, come, go),
        jax.ShapeDtypeStruct((BLOCKS, SLOTS, COLS), BF16),
        scratch,
        8 if rims else 7,
    )(rows, *tables(), weights, *([edges] if rims else []))


def by_row(flat, out, order):
    for y, place in enumerate(order):
        x = flat[pl.ds(y, MEM, stride=ROWS), :]
        x = jnp.concatenate([x, jnp.zeros((SLOTS - MEM, COLS), F32)], axis=0)
        out[place] = x.astype(BF16)


def pack_weights(loc, out, square, sheet):
    x = loc[...]
    for r in range(4):
        sheet[pl.ds(r, 8, stride=4), :] = turned(x, -BLOCKS * r)
    up = sheet[...]
    lane = lax.broadcasted_iota(jnp.int32, (BLOCKS, COLS), 1)
    row = lax.broadcasted_iota(jnp.int32, (BLOCKS, COLS), 0)
    next_row = jnp.where(row < BLOCKS - 1, pltpu.roll(up, BLOCKS - 1, 0), 0.0)
    down = jnp.where(lane == BLOCKS - 1, turned(next_row, BLOCKS - 1), turned(up, -1))
    both = jnp.concatenate([up, down, jnp.zeros((2 * BLOCKS, COLS), F32)], axis=0)
    square[...] = both.T
    for b in range(BLOCKS):
        sheet[b : b + 1, :] = square[BLOCKS - 1 - b : BLOCKS - b, :]
    h = jnp.where(lane < BLOCKS, square[:BLOCKS, :], jnp.where(lane < 2 * BLOCKS, sheet[...], 0.0))
    h = jnp.where(jnp.logical_and(row == 0, lane == 0), h, 0.5 * h)
    out[...] = h + turned(h, 2 * BLOCKS)


PIECE = 10
SMALL = 7


def first_body(
    alpha, ensemble, loc, cell, step, innovation, weight, std, control,
    out, tiles, edges, weights,
    alpha_v, ens_v, loc_v, cell_v, step_v, innovation_v, weight_v, std_v, control_v,
    flat, square, sheet, small_sem, alpha_sem, ens_sem,
):
    small = [
        pltpu.make_async_copy(a, b, small_sem.at[i])
        for i, (a, b) in enumerate(
            (
                (cell, cell_v),
                (step, step_v),
                (innovation, innovation_v),
                (weight, weight_v),
                (std, std_v),
                (control, control_v),
                (loc, loc_v),
            )
        )
    ]
    count = MEM // PIECE

    def pieces(source, target, sem):
        return [
            pltpu.make_async_copy(
                source.at[pl.ds(PIECE * i, PIECE)], target.at[pl.ds(PIECE * i, PIECE)], sem.at[i]
            )
            for i in range(count)
        ]

    from_alpha = pieces(alpha, alpha_v, alpha_sem)
    from_ensemble = pieces(ensemble, ens_v, ens_sem)
    for copy in small + from_alpha + from_ensemble:
        copy.start()
    for copy in small:
        copy.wait()
    observe(cell_v, step_v, innovation_v, weight_v, std_v, control_v, tiles, edges)
    pack_weights(loc_v, weights, square, sheet)
    for place in range(MEM + 4, SLOTS):
        flat[pl.ds(place, ROWS, stride=SLOTS), :] = jnp.zeros((ROWS, COLS), F32)
    for i, copy in enumerate(from_alpha):
        copy.wait()
        for m in range(PIECE * i, PIECE * i + PIECE):
            flat[pl.ds(m, ROWS, stride=SLOTS), :] = alpha_v[m]
    for copy in from_ensemble:
        copy.wait()
    for v in range(3):
        flat[pl.ds(MEM + v, ROWS, stride=SLOTS), :] = pack_slots(
            lambda m: ens_v[m, v].astype(F32), ROWS
        )
    flat[pl.ds(MEM + 3, ROWS, stride=SLOTS), :] = pack_extra(
        lambda m, v: ens_v[m, v].astype(F32), ROWS
    )
    for y, place in enumerate(FIRST):
        out[place] = flat[SLOTS * y : SLOTS * y + SLOTS, :].astype(BF16)


def first_step(alpha, ensemble, loc, cell, step, innovation, weight, std, control):
    far = pl.BlockSpec(memory_space=pltpu.HBM)
    near = pl.BlockSpec(memory_space=VMEM)
    line = (1, cell.shape[0])
    sems = pltpu.SemaphoreType.DMA
    return pl.pallas_call(
        first_body,
        out_shape=[
            jax.ShapeDtypeStruct((ROWS, SLOTS, COLS), BF16),
            jax.ShapeDtypeStruct((36, COLS), F32),
            jax.ShapeDtypeStruct((8, COLS), F32),
            jax.ShapeDtypeStruct((BLOCKS, COLS), F32),
        ],
        in_specs=[far] * 9,
        out_specs=[near] * 4,
        scratch_shapes=[
            VMEM(alpha.shape, F32),
            VMEM(ensemble.shape, BF16),
            VMEM((8, COLS), F32),
            VMEM(line, jnp.int32),
            VMEM(line, jnp.int32),
            VMEM(line, F32),
            VMEM(line, F32),
            VMEM(std.shape, F32),
            VMEM(control.shape, F32),
            VMEM((ROWS * SLOTS, COLS), F32),
            VMEM((COLS, COLS), F32),
            VMEM((BLOCKS, COLS), F32),
            sems((SMALL,)),
            sems((MEM // PIECE,)),
            sems((MEM // PIECE,)),
        ],
        compiler_params=pltpu.CompilerParams(vmem_limit_bytes=32 << 20),
    )(
        *[
            pltpu.with_memory_space_constraint(a, pltpu.HBM)
            for a in (
                alpha,
                ensemble,
                loc.reshape(8, COLS),
                *[a.reshape(line) for a in (cell, step, innovation, weight)],
                std,
                control,
            )
        ]
    )


def contract(ensemble, arrived, tiles, out, flat):
    own = lax.axis_index("grp")
    column = lax.axis_index(SP)
    unspread = math.sqrt(MEM * GROUPS - 1)
    for y, place in enumerate(SECOND):
        flat[SLOTS * y : SLOTS * y + SLOTS, :] = arrived[place].astype(F32)
    totals = [jnp.zeros((ROWS, COLS), F32)] * 3
    for m in range(MEM):
        field = flat[pl.ds(m, ROWS, stride=SLOTS), :]
        for v in range(3):
            totals[v] = totals[v] + ensemble[m, v].astype(F32) * field
    side = flat[pl.ds(MEM, ROWS, stride=SLOTS), :]
    right = (lax.broadcasted_iota(jnp.int32, (SLOTS, COLS), 1) & 15) < RIM

    def block(y):
        return flat[pl.ds(pl.multiple_of(SLOTS * (y & (BLOCKS - 1)), SLOTS), SLOTS), :]

    after = block(column + 1)
    before = block(column + BLOCKS - 1)
    rim = jnp.where(right, after, before)
    obs_rim = rim[MEM + 1 : MEM + 5]
    last = rim[MEM + 5 : MEM + 6]
    slot = slot_of((TILE_ROWS, COLS))
    static_rim = jnp.where(
        slot == 2,
        jnp.concatenate([turned(last, 16 * (2 - r)) for r in range(TILE_ROWS)], axis=0),
        turned(obs_rim, 32),
    )
    mine = jnp.right_shift(lax.broadcasted_iota(jnp.int32, (ROWS, COLS), 0), 2) == own

    def on_own_rows(tile):
        return jnp.where(mine, unspread * jnp.concatenate([tile] * GROUPS, axis=0), 0.0)

    parts = [
        (totals[v] + on_own_rows(tiles[24 + 4 * v : 28 + 4 * v, :])).astype(BF16)
        for v in range(3)
    ]
    side = side + on_own_rows(static_rim)
    side = jnp.where(slot_of((16, COLS)) < 4, side[:16], turned(side[16:], COLS // 2))
    parts.append(side.astype(BF16))
    parts.append(
        jnp.concatenate([tiles[:24, :], obs_rim, jnp.zeros((4, COLS), F32)], axis=0).astype(BF16)
    )
    payload = jnp.concatenate(parts, axis=0)
    out[...] = payload


def partial_sums(ensemble, arrived, tiles):
    return call(
        contract,
        jax.ShapeDtypeStruct((LOAD, COLS), BF16),
        [VMEM((ROWS * SLOTS, COLS), F32)],
        3,
    )(ensemble, arrived, tiles)


def add_pair(own, other, out):
    low = lax.axis_index("grp") < GROUPS // 2
    x = own[...].astype(F32)
    y = other[...].astype(F32)
    a, b = x[SUMMED:], y[SUMMED:]
    payload = jnp.concatenate(
        [x[:SUMMED] + y[:SUMMED], jnp.where(low, a, b), jnp.where(low, b, a)], axis=0
    ).astype(BF16)
    for g in range(GROUPS // 2):
        out[g] = payload


def pair_sums(own, other):
    return call(
        add_pair, jax.ShapeDtypeStruct((GROUPS // 2, LOAD + 32, COLS), BF16), (), 2
    )(own, other)


def observe(cell, step, innovation, weight, std, control, tiles, edges):
    where_row = jnp.right_shift(cell[...], 12) & (TILE_ROWS - 1)
    key = step[...] * TILE_ROWS + where_row
    column = cell[...] & (COLS - 1)
    w = weight[...]
    wd = w * innovation[...]
    n = 3 * TILE_ROWS
    count = w.shape[1]
    mine = lax.broadcasted_iota(jnp.int32, (n, count), 0) == key
    values = jnp.concatenate([jnp.where(mine, w, 0.0), jnp.where(mine, wd, 0.0)], axis=0)
    high = values.astype(BF16)
    rest = values - high.astype(F32)
    mid = rest.astype(BF16)
    low = (rest - mid.astype(F32)).astype(BF16)
    hot = (lax.broadcasted_iota(jnp.int32, (COLS, count), 0) == column).astype(F32).astype(BF16)
    pieces = lax.dot_general(
        jnp.concatenate([low.astype(F32), mid.astype(F32), high.astype(F32)], axis=0).astype(BF16),
        hot,
        (((1,), (1,)), ((), ())),
        preferred_element_type=F32,
    )
    total = pieces[: 2 * n] + pieces[2 * n : 4 * n] + pieces[4 * n :]
    static = [std[v] * control[v] for v in range(3)]
    tiles[:24, :] = total
    for v in range(3):
        tiles[24 + 4 * v : 28 + 4 * v, :] = static[v]
    slot = slot_of((TILE_ROWS, COLS))
    sums = jnp.zeros((TILE_ROWS, COLS), F32)
    for f in range(6):
        sums = jnp.where(slot == f, turned(total[4 * f : 4 * f + 4], 16 * f), sums)
    for v in range(2):
        sums = jnp.where(slot == 6 + v, turned(static[v], 16 * (6 + v)), sums)
    slot = slot_of((1, COLS))
    last = jnp.zeros((1, COLS), F32)
    for r in range(TILE_ROWS):
        last = jnp.where(slot == r, turned(static[2][r : r + 1], 16 * r), last)
    edges[...] = jnp.concatenate([sums, last, jnp.zeros((3, COLS), F32)], axis=0)


def window(arrived, ensemble, sent, tile, flat, sums):
    own = lax.axis_index("grp")
    spread = 1.0 / math.sqrt(MEM * GROUPS - 1)
    total = arrived[0, :SUMMED, :].astype(F32)
    for g in range(1, GROUPS // 2):
        total = total + arrived[g, :SUMMED, :].astype(F32)
    total = spread * total
    parts = [total[ROWS * v : ROWS * v + ROWS] for v in range(3)]
    side = total[3 * ROWS :]
    parts.append(jnp.concatenate([side, turned(side, COLS // 2)], axis=0))
    for g in range(GROUPS):
        x = arrived[THIRD[g % 4], SUMMED + 32 * (g // 4) : LOAD + 32 * (g // 4), :].astype(F32)
        for f in range(7):
            sums[f, TILE_ROWS * g : TILE_ROWS * g + TILE_ROWS, :] = x[4 * f : 4 * f + 4]
    lane = lax.broadcasted_iota(jnp.int32, (ROWS, COLS), 1)
    used = jnp.logical_or(lane < RIM, lane >= COLS - RIM)

    def wide(main, packed, place):
        rim = jnp.where(used, turned(packed, -16 * place), 0.0)
        return jnp.concatenate([main, rim], axis=1)

    row = lax.broadcasted_iota(jnp.int32, (ROWS, 2 * COLS), 0)
    rotation = 0.1 + 0.2 * (row.astype(F32) + 0.5) / ROWS
    down = row < ROWS - 1
    up = row > 0
    half_c = 0.5 * COURANT

    def dx(q):
        return half_c * (pltpu.roll(q, 2 * COLS - 1, 1) - pltpu.roll(q, 1, 1))

    def dy(q):
        below = jnp.where(down, pltpu.roll(q, ROWS - 1, 0), 0.0)
        above = jnp.where(up, pltpu.roll(q, 1, 0), 0.0)
        return half_c * (below - above)

    def forward(h, u, w):
        h1 = h - (dx(u) + dy(w))
        return h1, u - dx(h1) + rotation * w, w - dy(h1) - rotation * u

    def backward(bh, bu, bw):
        a = bh + (dx(bu) + dy(bw))
        return a, bu - rotation * bw + dx(a), bw + rotation * bu + dy(a)

    state = tuple(wide(parts[v], parts[3], v) for v in range(3))
    forcing = []
    for t in range(3):
        w_t = wide(sums[t], sums[6], t)
        v_t = wide(sums[3 + t], sums[6], 3 + t)
        forcing.append(w_t * state[0] - v_t)
        if t < 2:
            state = forward(*state)
    zero = jnp.zeros((ROWS, 2 * COLS), F32)
    bh, bu, bw = backward(forcing[2], zero, zero)
    bh, bu, bw = backward(bh + forcing[1], bu, bw)
    bh = bh + forcing[0]
    fin = [x[:, :COLS] for x in (bh, bu, bw)]
    for v in range(3):
        mine = fin[v][:TILE_ROWS]
        for g in range(1, GROUPS):
            mine = jnp.where(own == g, fin[v][TILE_ROWS * g : TILE_ROWS * g + TILE_ROWS], mine)
        tile[v] = mine
    for m in range(MEM):
        total = ensemble[m, 0].astype(F32) * fin[0]
        for v in range(1, 3):
            total = total + ensemble[m, v].astype(F32) * fin[v]
        flat[ROWS * m : ROWS * m + ROWS, :] = total
    by_row(flat, sent, FOURTH)


def assimilate(arrived, ensemble):
    return call(
        window,
        [
            jax.ShapeDtypeStruct((ROWS, SLOTS, COLS), BF16),
            jax.ShapeDtypeStruct((3, TILE_ROWS, COLS), F32),
        ],
        [VMEM((MEM * ROWS, COLS), F32), VMEM((7, ROWS, COLS), F32)],
        2,
    )(arrived, ensemble)


def add_alpha(alpha, arrived, tile, std, control, out, grad, flat):
    spread = 1.0 / math.sqrt(MEM * GROUPS - 1)
    for v in range(3):
        grad[v] = control[v] + std[v] * tile[v]
    for y, place in enumerate(FIFTH):
        flat[SLOTS * y : SLOTS * y + SLOTS, :] = arrived[place].astype(F32)
    for m in range(MEM):
        out[m] = alpha[m] + spread * flat[pl.ds(m, ROWS, stride=SLOTS), :]


def finish(alpha, arrived, tile, std, control):
    return call(
        add_alpha,
        [
            jax.ShapeDtypeStruct((MEM, ROWS, COLS), F32),
            jax.ShapeDtypeStruct((3, TILE_ROWS, COLS), F32),
        ],
        [VMEM((ROWS * SLOTS, COLS), F32)],
        5,
    )(alpha, arrived, tile, std, control)


def swap(x, axis, order):
    return lax.all_to_all(
        x, axis, split_axis=0, concat_axis=0, tiled=True, axis_index_groups=[order] if axis == SP else [order, [i + GROUPS // 2 for i in order]]
    )


def per_device(
    alpha, ensemble, static_std, control, loc_spectrum, obs_cell, obs_step, innovation, obs_weight
):
    sent, tiles, edges, weights = first_step(
        alpha, ensemble, loc_spectrum, obs_cell, obs_step, innovation, obs_weight, static_std, control
    )
    rows = swap(sent, SP, FIRST)
    localized = swap(localize(rows, weights, FIRST, SECOND, edges), SP, SECOND)
    own = partial_sums(ensemble, localized, tiles)
    other = lax.ppermute(own, "grp", [(i, (i + GROUPS // 2) % GROUPS) for i in range(GROUPS)])
    summed = swap(pair_sums(own, other), "grp", THIRD)
    sent, tile = assimilate(summed, ensemble)
    filtered = swap(localize(swap(sent, SP, FOURTH), weights, FOURTH, FIFTH), SP, FIFTH)
    return finish(alpha, filtered, tile, static_std, control)


def solution(mesh):
    both = P(("grp", SP))
    placed = (
        P("grp", None, SP),
        P("grp", None, None, SP),
        P(None, "grp", SP),
        P(None, "grp", SP),
        P(),
        both,
        both,
        both,
        both,
    )
    return jax.shard_map(
        per_device,
        mesh=mesh,
        in_specs=placed,
        out_specs=(P("grp", None, SP), P(None, "grp", SP)),
        check_vma=False,
    )
```
